32 devices in a mesh: gx: 8 (over y, x, core), gy: 4 (over z).
Axes of the slice: x: 2, y: 2, z: 4, core: 2. Of those that a mesh axis runs over, the one named last changes fastest.
Arguments:
- image_tokens: bfloat16 [16, 32, 32, 1152], P('gx', None, 'gy'), may hold values from -6 to 6
- text_tokens: bfloat16 [16, 80, 1152], P('gx', 'gy'), may hold values from -6 to 6
- image_skip: bfloat16 [16, 32, 32, 1152], P('gx', None, 'gy'), may hold values from -6 to 6
- text_skip: bfloat16 [16, 80, 1152], P('gx', 'gy'), may hold values from -6 to 6
- time_steps: int32 [16], P('gx'), may hold values from 0 to 999
- caption_len: int32 [16], P('gx'), may hold values from 1 to 77, as said below
- pred_grad: float32 [16, 4, 64, 64], P('gx', None, None, 'gy'), may hold values from -6 to 6
- text_grad: float32 [16, 80, 1152], P('gx', 'gy'), may hold values from -6 to 6
- w_skip: bfloat16 [2304, 1152], replicated, may hold values from -0.125 to 0.125
- b_skip: float32 [1152], replicated, may hold values from -1.8 to 1.8
- gain_attn: float32 [1152], replicated, may hold values from 0.5 to 1.5
- bias_attn: float32 [1152], replicated, may hold values from -1.8 to 1.8
- w_qkv: bfloat16 [1152, 3456], replicated, may hold values from -0.25 to 0.25
- w_proj: bfloat16 [1152, 1152], replicated, may hold values from -1 to 1
- b_proj: float32 [1152], replicated, may hold values from -1.8 to 1.8
- gain_mlp: float32 [1152], replicated, may hold values from 0.5 to 1.5
- bias_mlp: float32 [1152], replicated, may hold values from -1.8 to 1.8
- w_up: bfloat16 [1152, 4608], replicated, may hold values from -0.1875 to 0.1875
- b_up: float32 [4608], replicated, may hold values from -1.8 to 1.8
- w_down: bfloat16 [4608, 1152], replicated, may hold values from -0.09375 to 0.09375
- b_down: float32 [1152], replicated, may hold values from -1.8 to 1.8
- gain_head: float32 [1152], replicated, may hold values from 0.5 to 1.5
- bias_head: float32 [1152], replicated, may hold values from -1.8 to 1.8
- w_head: bfloat16 [1152, 16], replicated, may hold values from -0.1875 to 0.1875
- b_head: float32 [16], replicated, may hold values from -1.8 to 1.8
- w_conv: float32 [4, 4, 3, 3], replicated, may hold values from -1 to 1
- b_conv: float32 [4], replicated, may hold values from -1.8 to 1.8
Outputs:
- prediction: float32 [16, 4, 64, 64], P('gx', None, None, 'gy')
- text_out: bfloat16 [16, 80, 1152], P('gx', 'gy')
- grad_image: float32 [16, 32, 32, 1152], P('gx', None, 'gy')
- grad_text: float32 [16, 80, 1152], P('gx', 'gy')
- grad_image_skip: float32 [16, 32, 32, 1152], P('gx', None, 'gy')
- grad_text_skip: float32 [16, 80, 1152], P('gx', 'gy')
- grad_w_skip: float32 [2304, 1152], P(('gx', 'gy'))
- grad_b_skip: float32 [1152], P(('gx', 'gy'))
- grad_gain_attn: float32 [1152], P(('gx', 'gy'))
- grad_bias_attn: float32 [1152], P(('gx', 'gy'))
- grad_w_qkv: float32 [1152, 3456], P(('gx', 'gy'))
- grad_w_proj: float32 [1152, 1152], P(('gx', 'gy'))
- grad_b_proj: float32 [1152], P(('gx', 'gy'))
- grad_gain_mlp: float32 [1152], P(('gx', 'gy'))
- grad_bias_mlp: float32 [1152], P(('gx', 'gy'))
- grad_w_up: float32 [1152, 4608], P(('gx', 'gy'))
- grad_b_up: float32 [4608], P(('gx', 'gy'))
- grad_w_down: float32 [4608, 1152], P(('gx', 'gy'))
- grad_b_down: float32 [1152], P(('gx', 'gy'))
- grad_gain_head: float32 [1152], P(('gx', 'gy'))
- grad_bias_head: float32 [1152], P(('gx', 'gy'))
- grad_w_head: float32 [1152, 16], P(('gx', 'gy'))
- grad_b_head: float32 [16], replicated
- grad_w_conv: float32 [4, 4, 3, 3], replicated
- grad_b_conv: float32 [4], replicated
The draws below stay inside these ranges and needn't reach their ends.
Inputs may be any that keep to these rules, and one draw needn't show every extreme that they name: `caption_len`: caption tokens of each item that are attended to; some item has all 77.
All inputs are finite; a program needn't handle non-finite values.
Results may differ from the reference program's by a relative error of at most 0.017.
Values may be sent and summed in bfloat16 or wider, within the bound.
No kernel may reach another device: no remote copies, remote signals or barrier semaphores. Data moves between devices by JAX's collectives and lax.ppermute only.
A program may use at most 320 MiB of HBM per device.

```python
import math
import jax
import jax.numpy as jnp
from jax import lax

D = 1152
HEADS = 16
HEAD_DIM = 72
FF = 4608
LAT_CH = 4
PATCH = 2
GRID = 32
CAPTION = 77
ITEMS = 16
TEXT = 80
LAT = 64


def draw_caption_len(key, part):
    first, second = jax.random.split(key)
    lengths = jax.random.randint(first, (ITEMS,), 1, CAPTION + 1)
    chosen = jax.random.randint(second, (), 0, ITEMS)
    return jnp.where(jnp.arange(ITEMS) == chosen, CAPTION, lengths).astype(jnp.int32)


def plant(result, key, low, top_value):
    index_at = [jax.random.randint(jax.random.fold_in(key, axis), (), 0, length) for axis, length in enumerate(result.shape)]
    widest = result.shape.index(max(result.shape))
    beside = index_at[:widest] + [(index_at[widest] + 1) % result.shape[widest]] + index_at[widest + 1:]
    return result.at[tuple(index_at)].set(low).at[tuple(beside)].set(top_value)


def levels(rng, extent, cuts, least, top_value):
    factor_of = 1.0
    for axis_at, parts in cuts:
        steps = jax.random.uniform(jax.random.fold_in(jax.random.fold_in(rng, 6), axis_at), (parts,), jnp.float32, least / len(cuts), top_value / len(cuts))
        factor_of = factor_of * jnp.repeat(jnp.exp(steps), extent[axis_at] // parts).reshape((-1,) + (1,) * (len(extent) - 1 - axis_at))
    return factor_of


def scatter_about(stream_key, extent, width, most, pieces=(), kind=jnp.bfloat16):
    factor_of = levels(stream_key, extent, pieces, -0.22, 0.18) if pieces else 1.0
    array = jax.random.normal(stream_key, extent, jnp.float32) * width * factor_of
    return jnp.minimum(jnp.maximum(array, -most), most).astype(kind)


def setup_inputs(seed: int = 0) -> dict:
    key_of = jax.random.split(jax.random.key(seed), 28)
    return {
        "image_tokens": scatter_about(key_of[0], (ITEMS, GRID, GRID, D), 1.0, 6.0, ((0, 8), (2, 4))),
        "text_tokens": scatter_about(key_of[1], (ITEMS, TEXT, D), 1.0, 6.0, ((0, 8), (1, 4))),
        "image_skip": scatter_about(key_of[2], (ITEMS, GRID, GRID, D), 1.0, 6.0, ((0, 8), (2, 4))),
        "text_skip": scatter_about(key_of[3], (ITEMS, TEXT, D), 1.0, 6.0, ((0, 8), (1, 4))),
        "time_steps": plant(jax.random.randint(key_of[4], (ITEMS,), 0, 1000), jax.random.fold_in(key_of[4], 1), 0, 999).astype(jnp.int32),
        "caption_len": draw_caption_len(jax.random.fold_in(key_of[27], 71), 0),
        "pred_grad": scatter_about(key_of[6], (ITEMS, LAT_CH, LAT, LAT), 1.0, 6.0, ((0, 8), (3, 4)), jnp.float32),
        "text_grad": scatter_about(key_of[7], (ITEMS, TEXT, D), 1.0, 6.0, ((0, 8), (1, 4)), jnp.float32),
        "w_skip": scatter_about(key_of[8], (2 * D, D), (2 * D) ** -0.5, 0.125),
        "b_skip": scatter_about(key_of[9], (D,), 0.3, 1.8, (), jnp.float32),
        "gain_attn": jnp.clip(1.0 + 0.1 * jax.random.normal(key_of[10], (D,), jnp.float32), 0.5, 1.5),
        "bias_attn": scatter_about(key_of[11], (D,), 0.3, 1.8, (), jnp.float32),
        "w_qkv": scatter_about(key_of[12], (D, 3 * D), (D // 2) ** -0.5, 0.25),
        "w_proj": scatter_about(key_of[13], (D, D), (D // 32) ** -0.5, 1.0),
        "b_proj": scatter_about(key_of[14], (D,), 0.3, 1.8, (), jnp.float32),
        "gain_mlp": jnp.clip(1.0 + 0.1 * jax.random.normal(key_of[15], (D,), jnp.float32), 0.5, 1.5),
        "bias_mlp": scatter_about(key_of[16], (D,), 0.3, 1.8, (), jnp.float32),
        "w_up": scatter_about(key_of[17], (D, FF), D ** -0.5, 0.1875),
        "b_up": scatter_about(key_of[18], (FF,), 0.3, 1.8, (), jnp.float32),
        "w_down": scatter_about(key_of[19], (FF, D), FF ** -0.5, 0.09375),
        "b_down": scatter_about(key_of[20], (D,), 0.3, 1.8, (), jnp.float32),
        "gain_head": jnp.clip(1.0 + 0.1 * jax.random.normal(key_of[21], (D,), jnp.float32), 0.5, 1.5),
        "bias_head": scatter_about(key_of[22], (D,), 0.3, 1.8, (), jnp.float32),
        "w_head": scatter_about(key_of[23], (D, LAT_CH * PATCH * PATCH), D ** -0.5, 0.1875),
        "b_head": scatter_about(key_of[24], (LAT_CH * PATCH * PATCH,), 0.3, 1.8, (), jnp.float32),
        "w_conv": scatter_about(key_of[25], (LAT_CH, LAT_CH, 3, 3), (LAT_CH * 9) ** -0.5, 1.0, (), jnp.float32),
        "b_conv": scatter_about(key_of[26], (LAT_CH,), 0.3, 1.8, (), jnp.float32),
    }


@jax.custom_vjp
def low(v):
    return lax.optimization_barrier(v.astype(jnp.bfloat16)).astype(jnp.float32)

@jax.custom_vjp
def low_back(v):
    return v

def low_keep(v):
    return (low(v), None)

def low_pass(kept, grad):
    return (grad,)

def back_keep(v):
    return (v, None)

def back_low(kept, grad):
    return (low(grad),)
low.defvjp(low_keep, low_pass)
low_back.defvjp(back_keep, back_low)
EPSILON = 1e-05
HIGHEST = lax.Precision.HIGHEST

def matmul(left, right):
    return jnp.dot(left, right, precision=HIGHEST, preferred_element_type=jnp.float32)

def layer_norm(values, gain, bias):
    centre = lax.optimization_barrier(jnp.mean(values, axis=-1, keepdims=True))
    centred = values - centre
    variance = lax.optimization_barrier(jnp.mean(centred * centred, axis=-1, keepdims=True))
    return centred * lax.rsqrt(variance + EPSILON) * gain + bias

def time_embedding(time_steps):
    half_width = D // 2
    freqs = jnp.exp(-math.log(10000.0) * jnp.arange(half_width, dtype=jnp.float32) / half_width)
    angles = time_steps.astype(jnp.float32)[:, None] * freqs[None, :]
    return jnp.concatenate([jnp.cos(angles), jnp.sin(angles)], axis=1)

def reference(image_tokens, text_tokens, image_skip, text_skip, time_steps, caption_len, pred_grad, text_grad, w_skip, b_skip, gain_attn, bias_attn, w_qkv, w_proj, b_proj, gain_mlp, bias_mlp, w_up, b_up, w_down, b_down, gain_head, bias_head, w_head, b_head, w_conv, b_conv):
    length_all = TEXT + GRID * GRID
    scale = HEAD_DIM ** (-0.5)
    embed = time_embedding(time_steps)
    positions = jnp.arange(length_all, dtype=jnp.int32)
    allowed_all = (positions[None, :] >= TEXT) | (positions[None, :] <= caption_len[:, None])
    first_row = (jnp.arange(TEXT, dtype=jnp.int32) == 0).astype(jnp.float32)

    def attend(packed):
        queries, keys, values, allowed = packed
        queries = queries.reshape(length_all, HEADS, HEAD_DIM)
        keys = keys.reshape(length_all, HEADS, HEAD_DIM)
        values = values.reshape(length_all, HEADS, HEAD_DIM)
        scores = low_back(jnp.einsum('qhe,khe->hqk', queries, keys, precision=HIGHEST) * scale)
        scores = jnp.where(allowed[None, None, :], scores, -1e+30)
        largest = lax.optimization_barrier(jnp.max(scores, axis=2, keepdims=True))
        weights = jnp.exp(scores - largest)
        probs = weights / lax.optimization_barrier(jnp.sum(weights, axis=2, keepdims=True))
        mixed = jnp.einsum('hqk,khe->qhe', low(probs), values, precision=HIGHEST)
        return mixed.reshape(length_all, D)

    def forward(image_in, text_in, image_sk, text_sk, w_skip, b_skip, gain_attn, bias_attn, w_qkv, w_proj, b_proj, gain_mlp, bias_mlp, w_up, b_up, w_down, b_down, gain_head, bias_head, w_head, b_head, w_conv, b_conv):
        text_rows = text_in + first_row[None, :, None] * embed[:, None, :]
        tokens = jnp.concatenate([text_rows, image_in.reshape(ITEMS, GRID * GRID, D)], axis=1)
        skips = jnp.concatenate([text_sk, image_sk.reshape(ITEMS, GRID * GRID, D)], axis=1)
        joined = low(jnp.concatenate([tokens, skips], axis=2).reshape(ITEMS * length_all, 2 * D))
        resid = low_back(matmul(joined, w_skip)) + b_skip
        normed = low(layer_norm(resid, gain_attn, bias_attn))
        projected = low(low_back(matmul(normed, w_qkv))).reshape(ITEMS, length_all, 3 * D)
        mixed = lax.map(jax.checkpoint(attend), (projected[:, :, :D], projected[:, :, D:2 * D], projected[:, :, 2 * D:], allowed_all))
        mixed = low(low_back(mixed.reshape(ITEMS * length_all, D)))
        resid = resid + low_back(matmul(mixed, w_proj)) + b_proj
        normed = low(layer_norm(resid, gain_mlp, bias_mlp))
        hidden = low_back(matmul(normed, w_up) + b_up)
        hidden = low(jax.nn.gelu(hidden, approximate=False))
        resid = resid + low_back(matmul(hidden, w_down)) + b_down
        resid = resid.reshape(ITEMS, length_all, D)
        text_out = resid[:, :TEXT]
        image_out = resid[:, TEXT:].reshape(ITEMS * GRID * GRID, D)
        normed = low(layer_norm(image_out, gain_head, bias_head))
        patches = matmul(normed, w_head) + b_head
        latent = patches.reshape(ITEMS, GRID, GRID, PATCH, PATCH, LAT_CH)
        latent = jnp.transpose(latent, (0, 5, 1, 3, 2, 4)).reshape(ITEMS, LAT_CH, LAT, LAT)
        padded = jnp.pad(latent, ((0, 0), (0, 0), (1, 1), (1, 1)))
        prediction = jnp.zeros((ITEMS, LAT_CH, LAT, LAT), jnp.float32) + b_conv[None, :, None, None]
        for row_off in range(3):
            for col_off in range(3):
                prediction = prediction + jnp.einsum('oi,bihw->bohw', w_conv[:, :, row_off, col_off], padded[:, :, row_off:row_off + LAT, col_off:col_off + LAT], precision=HIGHEST)
        return (prediction, text_out)
    floats = [image_tokens, text_tokens, image_skip, text_skip, w_skip, b_skip, gain_attn, bias_attn, w_qkv, w_proj, b_proj, gain_mlp, bias_mlp, w_up, b_up, w_down, b_down, gain_head, bias_head, w_head, b_head, w_conv, b_conv]
    floats = [item.astype(jnp.float32) for item in floats]
    outputs, pull = jax.vjp(forward, *floats)
    grads = pull((pred_grad.astype(jnp.float32), text_grad.astype(jnp.float32)))
    return (outputs[0], outputs[1].astype(jnp.bfloat16), grads[0], grads[1], grads[2], grads[3], grads[4], grads[5], grads[6], grads[7], grads[8], grads[9], grads[10], grads[11], grads[12], grads[13], grads[14], grads[15], grads[16], grads[17], grads[18], grads[19], grads[20], grads[21], grads[22])
```

```python
from functools import partial
import math

import jax
import jax.numpy as jnp
from jax import lax
from jax.sharding import PartitionSpec as P

HEADS = 16
HEAD_DIM = 72
LAT_CH = 4
PATCH = 2

EPSILON = 1e-05
HIGHEST = lax.Precision.HIGHEST
F32 = jnp.float32
BF16 = jnp.bfloat16


def bits_of(count):
    bits = count.bit_length() - 1
    assert 1 << bits == count
    return bits


def with_halo(block, axis, dim, width):
    count = lax.axis_size(axis)
    forward = [(i, i + 1) for i in range(count - 1)]
    backward = [(target, source) for source, target in forward]
    low = lax.ppermute(
        lax.slice_in_dim(block, block.shape[dim] - width, None, axis=dim), axis, forward
    )
    high = lax.ppermute(lax.slice_in_dim(block, 0, width, axis=dim), axis, backward)
    return jnp.concatenate([low, block, high], axis=dim)


def layer_norm(values, gain, bias):
    centre = jnp.mean(values, axis=-1, keepdims=True)
    centred = values - centre
    variance = jnp.mean(centred * centred, axis=-1, keepdims=True)
    return centred * lax.rsqrt(variance + EPSILON) * gain + bias


def time_embedding(time_steps, model_width):
    half_width = model_width // 2
    freqs = jnp.exp(-math.log(10000.0) * jnp.arange(half_width, dtype=F32) / half_width)
    angles = time_steps.astype(F32)[:, None] * freqs[None, :]
    return jnp.concatenate([jnp.cos(angles), jnp.sin(angles)], axis=1)


def project(rows, weight):
    return jnp.einsum("rd,de->re", rows, weight, preferred_element_type=F32)


def weight_grad(rows, grads):
    return jnp.einsum("rd,re->de", rows, grads, preferred_element_type=F32)


def back_project(grads, weight):
    return jnp.einsum("re,de->rd", grads, weight, preferred_element_type=F32)


class Regroup:
    def __init__(self):
        self.gx, self.gy = lax.axis_size("gx"), lax.axis_size("gy")
        self.ratio = self.gy // 4
        assert self.ratio * 4 == self.gy and self.gx % 2 == 0
        core, z = lax.axis_index("gx") % 2, lax.axis_index("gy")
        self.parity = z % 2
        self.item = z // self.ratio
        self.slot = (z % self.ratio) * 2 + core
        self.holders = 2 * self.ratio
        self.perms = []
        for turn in range(2):
            pairs = []
            for gx in range(self.gx):
                pair, c = gx // 2, gx % 2
                for z in range(self.gy):
                    f = (z & 1) ^ turn
                    item, d = 2 * c + f, z // 2
                    to_z, to_c = item * self.ratio + d // 2, d % 2
                    pairs.append((gx * self.gy + z, (2 * pair + to_c) * self.gy + to_z))
            self.perms.append(pairs)

    def there(self, blocks):
        out = []
        for turn in range(2):
            send = lax.dynamic_index_in_dim(blocks, self.parity ^ turn, 0, keepdims=False)
            out.append(lax.ppermute(send, ("gx", "gy"), self.perms[turn]))
        return out

    def back(self, first, second):
        got = [
            lax.ppermute(part, ("gx", "gy"), [(b, a) for a, b in self.perms[turn]])
            for turn, part in enumerate((first, second))
        ]
        even = self.parity == 0
        return jnp.stack([jnp.where(even, got[0], got[1]), jnp.where(even, got[1], got[0])])

    def share(self, rows, step):
        pairs = []
        for gx in range(self.gx):
            pair, c = gx // 2, gx % 2
            for z in range(self.gy):
                base, d = z // self.ratio * self.ratio, (z % self.ratio) * 2 + c
                to = (d + step) % self.holders
                pairs.append(
                    (gx * self.gy + z, (2 * pair + to % 2) * self.gy + base + to // 2)
                )
        return lax.ppermute(rows, ("gx", "gy"), pairs)

    def block_z(self, step, turn):
        d = (self.slot - step) % self.holders
        return 2 * d + ((self.item % 2) ^ turn)


def scatter_sum(part, order, wire):
    sizes = {axis: lax.axis_size(axis) for axis in ("gx", "gy")}
    dims = [(axis, bit) for axis in ("gx", "gy") for bit in reversed(range(bits_of(sizes[axis])))]
    rows, rest = part.shape[0] >> len(dims), part.shape[1:]
    for axis, bit in order:
        place = dims.index((axis, bit))
        before, after = 1 << place, 1 << (len(dims) - place - 1)
        part = part.reshape((before, 2, after * rows) + rest)
        mine = (lax.axis_index(axis) >> bit) & 1
        send = lax.dynamic_index_in_dim(part, 1 - mine, 1, keepdims=False)
        keep = lax.dynamic_index_in_dim(part, mine, 1, keepdims=False)
        got = lax.ppermute(send, axis, [(i, i ^ (1 << bit)) for i in range(sizes[axis])])
        part = (keep.astype(F32) + got.astype(F32)).astype(wire)
        part = part.reshape((before * after * rows,) + rest)
        dims.pop(place)
    return part


def orders():
    gx = list(range(bits_of(lax.axis_size("gx"))))
    gy = list(range(bits_of(lax.axis_size("gy"))))
    first = [("gx", b) for b in gx] + [("gy", b) for b in gy]
    second = [("gx", 0)] + [("gx", b) for b in reversed(gx[1:])] + [("gy", b) for b in gy]
    return first, second


def matrix_grad(rows, grads, cut, order_pair):
    pieces = []
    for part, order in zip((grads[:, :cut], grads[:, cut:]), order_pair):
        pieces.append(scatter_sum(weight_grad(rows, part).astype(BF16), order, BF16))
    return jnp.concatenate(pieces, axis=1).astype(F32)


def per_device(
    image_tokens,
    text_tokens,
    image_skip,
    text_skip,
    time_steps,
    caption_len,
    pred_grad,
    text_grad,
    w_skip,
    b_skip,
    gain_attn,
    bias_attn,
    w_qkv,
    w_proj,
    b_proj,
    gain_mlp,
    bias_mlp,
    w_up,
    b_up,
    w_down,
    b_down,
    gain_head,
    bias_head,
    w_head,
    b_head,
    w_conv,
    b_conv,
):
    item_count, text_dev, width = text_tokens.shape
    grid_rows, grid_cols = (image_tokens.shape[1], image_tokens.shape[2])
    image_dev = grid_rows * grid_cols
    assert item_count == 2
    block = -(-(image_dev + text_dev) // 16) * 16
    text_pad = block - image_dev
    rows = 2 * block
    go = Regroup()
    scale = HEAD_DIM ** (-0.5)
    order_pair = orders()
    devices = go.gx * go.gy

    lat_shape = pred_grad.shape
    lat_rows, lat_cols = (lat_shape[2], lat_shape[3])
    grad_pad = jnp.pad(with_halo(pred_grad, "gy", 3, 1), ((0, 0), (0, 0), (1, 1), (0, 0)))
    grad_latent = jnp.zeros(lat_shape, F32)
    for row_off in range(3):
        for col_off in range(3):
            grad_latent = grad_latent + jnp.einsum(
                "oi,bohw->bihw",
                w_conv[:, :, row_off, col_off],
                grad_pad[
                    :, :, 2 - row_off : 2 - row_off + lat_rows, 2 - col_off : 2 - col_off + lat_cols
                ],
                precision=HIGHEST,
            )
    grad_patches = jnp.transpose(
        grad_latent.reshape(item_count, LAT_CH, grid_rows, PATCH, grid_cols, PATCH),
        (0, 2, 4, 3, 5, 1),
    ).reshape(item_count, image_dev, LAT_CH * PATCH * PATCH)
    grad_b_head = jnp.sum(grad_patches, axis=(0, 1))
    grad_b_conv = jnp.sum(pred_grad, axis=(0, 2, 3))

    slots = lax.axis_index("gy") * text_dev + jnp.arange(text_dev, dtype=jnp.int32)
    first_row = (slots == 0).astype(F32)
    embed = time_embedding(time_steps, width)
    text_in = (text_tokens.astype(F32) + first_row[None, :, None] * embed[:, None, :]).astype(BF16)

    def rows_of(image, text):
        return jnp.concatenate(
            [
                image.reshape(item_count, image_dev, width),
                jnp.pad(text, ((0, 0), (0, text_pad - text_dev), (0, 0))),
            ],
            axis=1,
        )

    joined_here = jnp.concatenate(
        [rows_of(image_tokens, text_in), rows_of(image_skip, text_skip)], axis=2
    )
    resid_here = (
        project(joined_here.reshape(rows, 2 * width), w_skip) + b_skip
    ).astype(BF16)
    resid = jnp.concatenate(go.there(resid_here.reshape(2, block, width)), axis=0).astype(F32)
    gate, joined_late, text_grad, grad_patches, caption = lax.optimization_barrier(
        (resid, joined_here, text_grad, grad_patches, caption_len.astype(F32))
    )
    resid = gate
    joined = jnp.concatenate(go.there(joined_late), axis=0)
    patch_rows = -(-grad_patches.shape[1] * grad_patches.shape[2] // width)
    flat = grad_patches.reshape(2, -1)
    flat = jnp.pad(flat, ((0, 0), (0, patch_rows * width - flat.shape[1])))
    message = jnp.concatenate(
        [
            text_grad,
            flat.reshape(2, patch_rows, width),
            jnp.broadcast_to(caption[:, None, None], (2, 1, width)),
        ],
        axis=1,
    )
    message = go.there(message)
    text_grad_rows = [part[:text_dev] for part in message]
    grad_patches = jnp.concatenate(
        [
            part[text_dev : text_dev + patch_rows].reshape(-1)[: image_dev * 16].reshape(-1, 16)
            for part in message
        ],
        axis=0,
    )
    caption = message[0][-1, 0].astype(jnp.int32)

    normed_attn, attn_norm_back = jax.vjp(layer_norm, resid, gain_attn, bias_attn)
    normed = normed_attn.astype(BF16)
    qkv = project(normed, w_qkv).astype(BF16)
    queries, key_values = qkv[:, :width], qkv[:, width:]
    shared = [key_values] + [go.share(key_values, step) for step in range(1, go.holders)]
    allowed = []
    for step in range(go.holders):
        for turn in range(2):
            slot = go.block_z(step, turn) * text_dev + jnp.arange(text_pad)
            inside = (jnp.arange(text_pad) < text_dev) & (slot <= caption)
            allowed += [jnp.ones((image_dev,), jnp.bool_), inside]
    allowed = jnp.concatenate(allowed)
    key_values = jnp.concatenate(shared, axis=0)
    key_rows = rows * go.holders

    query_heads = queries.reshape(rows, HEADS, HEAD_DIM)
    key_heads = key_values[:, :width].reshape(key_rows, HEADS, HEAD_DIM)
    value_heads = key_values[:, width:].reshape(key_rows, HEADS, HEAD_DIM)

    def scores_of():
        raw = jnp.einsum("ihe,jhe->hij", query_heads, key_heads, preferred_element_type=F32) * scale
        return jnp.where(allowed[None, None, :], raw, -1e30)

    scores = scores_of()
    largest = jnp.max(scores, axis=2, keepdims=True)
    expo = jnp.exp(scores - largest)
    totals = jnp.sum(expo, axis=2, keepdims=True)
    probs = expo / totals
    log_total = largest + jnp.log(totals)
    mixed = jnp.einsum("hij,jhe->ihe", probs.astype(BF16), value_heads, preferred_element_type=F32)
    mixed = mixed.reshape(rows, width).astype(BF16)

    resid_two = resid + project(mixed, w_proj) + b_proj
    normed_mlp, mlp_norm_back = jax.vjp(layer_norm, resid_two, gain_mlp, bias_mlp)
    normed_two = normed_mlp.astype(BF16)
    pre_act = project(normed_two, w_up) + b_up
    activated, gelu_back = jax.vjp(partial(jax.nn.gelu, approximate=False), pre_act)
    hidden = activated.astype(BF16)
    resid_three = resid_two + project(hidden, w_down) + b_down

    def image_of(values):
        return jnp.concatenate([values[:image_dev], values[block : block + image_dev]], axis=0)

    def text_of(values):
        return [values[image_dev : image_dev + text_dev], values[block + image_dev : block + image_dev + text_dev]]

    text_out = go.back(*[part.astype(BF16) for part in text_of(resid_three)])
    normed_head, head_norm_back = jax.vjp(layer_norm, image_of(resid_three), gain_head, bias_head)
    head_in = normed_head.astype(BF16)
    patches = project(head_in, w_head) + b_head
    patches = go.back(patches[:image_dev], patches[image_dev:])

    patch_grid = patches.reshape(item_count, grid_rows, grid_cols, PATCH, PATCH, LAT_CH)
    latent = jnp.transpose(patch_grid, (0, 5, 1, 3, 2, 4)).reshape(lat_shape)
    padded = jnp.pad(with_halo(latent, "gy", 3, 1), ((0, 0), (0, 0), (1, 1), (0, 0)))
    prediction = jnp.zeros(lat_shape, F32) + b_conv[None, :, None, None]
    conv_taps = []
    for row_off in range(3):
        for col_off in range(3):
            window = padded[:, :, row_off : row_off + lat_rows, col_off : col_off + lat_cols]
            prediction = prediction + jnp.einsum(
                "oi,bihw->bohw", w_conv[:, :, row_off, col_off], window, precision=HIGHEST
            )
            conv_taps.append(jnp.einsum("bohw,bihw->oi", pred_grad, window, precision=HIGHEST))
    grad_w_conv = jnp.stack(conv_taps, axis=-1)

    grad_w_head = jnp.einsum("rd,ro->do", head_in.astype(F32), grad_patches, precision=HIGHEST)
    grad_normed_head = jnp.einsum("ro,do->rd", grad_patches, w_head.astype(F32), precision=HIGHEST)
    grad_image_out, grad_gain_head, grad_bias_head = head_norm_back(grad_normed_head)
    text_padding = ((0, text_pad - text_dev), (0, 0))
    grad_three = jnp.concatenate(
        [
            grad_image_out[:image_dev],
            jnp.pad(text_grad_rows[0], text_padding),
            grad_image_out[image_dev:],
            jnp.pad(text_grad_rows[1], text_padding),
        ],
        axis=0,
    )
    grad_b_down = jnp.sum(grad_three, axis=0)
    down_in = grad_three.astype(BF16)
    grad_w_down = matrix_grad(hidden, down_in, 640, order_pair)
    (grad_pre,) = gelu_back(back_project(down_in, w_down))
    pre_low = grad_pre.astype(BF16)
    grad_b_up = jnp.sum(pre_low.astype(F32), axis=0)
    grad_w_up = matrix_grad(normed_two, pre_low, 2304, order_pair)
    grad_two, grad_gain_mlp, grad_bias_mlp = mlp_norm_back(back_project(pre_low, w_up))
    grad_two = grad_two + grad_three
    grad_b_proj = jnp.sum(grad_two, axis=0)
    proj_in = grad_two.astype(BF16)
    grad_w_proj = matrix_grad(mixed, proj_in, 640, order_pair)
    grad_mixed = back_project(proj_in, w_proj).astype(BF16)
    grad_mixed_heads = grad_mixed.reshape(rows, HEADS, HEAD_DIM)
    grad_dots = jnp.einsum("ihe,jhe->hij", grad_mixed_heads, value_heads, preferred_element_type=F32)
    probs_again = jnp.exp(scores_of() - log_total)
    row_delta = jnp.sum(probs_again * grad_dots, axis=2, keepdims=True)
    grad_scores = (probs_again * (grad_dots - row_delta)).astype(BF16)
    grad_queries = (
        jnp.einsum("hij,jhe->ihe", grad_scores, key_heads, preferred_element_type=F32) * scale
    ).reshape(rows, width)
    probs_low = probs_again.astype(BF16)
    key_grad = (
        jnp.einsum("hij,ihe->jhe", grad_scores, query_heads, preferred_element_type=F32) * scale
    )
    value_grad = jnp.einsum("hij,ihe->jhe", probs_low, grad_mixed_heads, preferred_element_type=F32)
    grad_kv = jnp.concatenate(
        [key_grad.reshape(key_rows, width), value_grad.reshape(key_rows, width)], axis=1
    ).astype(BF16)
    grad_kv_sum = grad_kv[:rows].astype(F32)
    for step in range(1, go.holders):
        part = go.share(grad_kv[step * rows : (step + 1) * rows], go.holders - step)
        grad_kv_sum = grad_kv_sum + part.astype(F32)
    grad_qkv = jnp.concatenate([grad_queries, grad_kv_sum], axis=1).astype(BF16)
    grad_w_qkv = matrix_grad(normed, grad_qkv, 1792, order_pair)
    grad_one, grad_gain_attn, grad_bias_attn = attn_norm_back(back_project(grad_qkv, w_qkv))
    grad_one = grad_one + grad_two
    grad_b_skip = jnp.sum(grad_one, axis=0)
    skip_in = grad_one.astype(BF16)
    grad_w_skip = matrix_grad(joined, skip_in, 640, order_pair)
    skip_here = go.back(skip_in[:block], skip_in[block:])
    grad_joined = back_project(skip_here.reshape(rows, width), w_skip).reshape(2, block, 2 * width)
    image_shape = image_tokens.shape
    grad_image = grad_joined[:, :image_dev, :width].reshape(image_shape)
    grad_image_skip = grad_joined[:, :image_dev, width:].reshape(image_shape)
    grad_text = grad_joined[:, image_dev : image_dev + text_dev, :width]
    grad_text_skip = grad_joined[:, image_dev : image_dev + text_dev, width:]

    vectors = (
        grad_b_skip,
        grad_gain_attn,
        grad_bias_attn,
        grad_b_proj,
        grad_gain_mlp,
        grad_bias_mlp,
        grad_b_up,
        grad_b_down,
        grad_gain_head,
        grad_bias_head,
        grad_w_head,
    )
    whole = jnp.concatenate([grad_b_head, grad_w_conv.reshape(-1), grad_b_conv])
    packed = [v.reshape(devices, -1) for v in vectors]
    packed.append(jnp.broadcast_to(whole[None], (devices, whole.shape[0])))
    packed = jnp.concatenate(packed, axis=1)
    packed = jnp.pad(packed, ((0, 0), (0, -packed.shape[1] % 128)))
    packed = scatter_sum(packed, order_pair[0], F32)[0]
    small = []
    start = 0
    for v in vectors:
        size = v.size // devices
        small.append(packed[start : start + size])
        start += size
    small[-1] = small[-1].reshape(-1, grad_w_head.shape[1])
    whole = packed[start : start + whole.shape[0]]
    patch_size = grad_b_head.shape[0]
    taps = grad_w_conv.size
    return (
        prediction,
        text_out,
        grad_image,
        grad_text,
        grad_image_skip,
        grad_text_skip,
        grad_w_skip,
        small[0],
        small[1],
        small[2],
        grad_w_qkv,
        grad_w_proj,
        small[3],
        small[4],
        small[5],
        grad_w_up,
        small[6],
        grad_w_down,
        small[7],
        small[8],
        small[9],
        small[10],
        whole[:patch_size],
        whole[patch_size : patch_size + taps].reshape(LAT_CH, LAT_CH, 3, 3),
        whole[patch_size + taps :],
    )


def solution(mesh):
    rows = P(("gx", "gy"))
    image = P("gx", None, "gy", None)
    text = P("gx", "gy", None)
    latent = P("gx", None, None, "gy")
    return jax.shard_map(
        per_device,
        mesh=mesh,
        in_specs=(image, text, image, text, P("gx"), P("gx"), latent, text) + (P(),) * 19,
        out_specs=(latent, text, image, text, image, text) + (rows,) * 16 + (P(),) * 3,
        check_vma=False,
    )
```

```python
from functools import partial
import math

import jax
import jax.numpy as jnp
from jax import lax
from jax.experimental import pallas as pl
from jax.experimental.pallas import tpu as pltpu
from jax.sharding import PartitionSpec as P

HEADS = 16
HEAD_DIM = 72
LAT_CH = 4
PATCH = 2

EPSILON = 1e-05
HIGHEST = lax.Precision.HIGHEST
F32 = jnp.float32
BF16 = jnp.bfloat16


def bits_of(count):
    bits = count.bit_length() - 1
    assert 1 << bits == count
    return bits


def with_halo(block, axis, dim, width):
    count = lax.axis_size(axis)
    forward = [(i, i + 1) for i in range(count - 1)]
    backward = [(target, source) for source, target in forward]
    low = lax.ppermute(
        lax.slice_in_dim(block, block.shape[dim] - width, None, axis=dim), axis, forward
    )
    high = lax.ppermute(lax.slice_in_dim(block, 0, width, axis=dim), axis, backward)
    return jnp.concatenate([low, block, high], axis=dim)


def layer_norm(values, gain, bias):
    centre = jnp.mean(values, axis=-1, keepdims=True)
    centred = values - centre
    variance = jnp.mean(centred * centred, axis=-1, keepdims=True)
    return centred * lax.rsqrt(variance + EPSILON) * gain + bias


def time_embedding(time_steps, model_width):
    half_width = model_width // 2
    freqs = jnp.exp(-math.log(10000.0) * jnp.arange(half_width, dtype=F32) / half_width)
    angles = time_steps.astype(F32)[:, None] * freqs[None, :]
    return jnp.concatenate([jnp.cos(angles), jnp.sin(angles)], axis=1)


def project(rows, weight):
    return jnp.einsum("rd,de->re", rows, weight, preferred_element_type=F32)


def weight_grad(rows, grads):
    return jnp.einsum("rd,re->de", rows, grads, preferred_element_type=F32)


def back_project(grads, weight):
    return jnp.einsum("re,de->rd", grads, weight, preferred_element_type=F32)


class Regroup:
    def __init__(self):
        self.gx, self.gy = lax.axis_size("gx"), lax.axis_size("gy")
        self.ratio = self.gy // 4
        assert self.ratio * 4 == self.gy and self.gx % 2 == 0
        core, z = lax.axis_index("gx") % 2, lax.axis_index("gy")
        self.parity = z % 2
        self.item = z // self.ratio
        self.slot = (z % self.ratio) * 2 + core
        self.holders = 2 * self.ratio
        self.perms = []
        for turn in range(2):
            pairs = []
            for gx in range(self.gx):
                pair, c = gx // 2, gx % 2
                for z in range(self.gy):
                    f = (z & 1) ^ turn
                    item, d = 2 * c + f, z // 2
                    to_z, to_c = item * self.ratio + d // 2, d % 2
                    pairs.append((gx * self.gy + z, (2 * pair + to_c) * self.gy + to_z))
            self.perms.append(pairs)

    def there(self, blocks):
        out = []
        for turn in range(2):
            send = lax.dynamic_index_in_dim(blocks, self.parity ^ turn, 0, keepdims=False)
            out.append(lax.ppermute(send, ("gx", "gy"), self.perms[turn]))
        return out

    def back(self, first, second):
        got = [
            lax.ppermute(part, ("gx", "gy"), [(b, a) for a, b in self.perms[turn]])
            for turn, part in enumerate((first, second))
        ]
        even = self.parity == 0
        return jnp.stack([jnp.where(even, got[0], got[1]), jnp.where(even, got[1], got[0])])

    def share(self, rows, step):
        pairs = []
        for gx in range(self.gx):
            pair, c = gx // 2, gx % 2
            for z in range(self.gy):
                base, d = z // self.ratio * self.ratio, (z % self.ratio) * 2 + c
                to = (d + step) % self.holders
                pairs.append(
                    (gx * self.gy + z, (2 * pair + to % 2) * self.gy + base + to // 2)
                )
        return lax.ppermute(rows, ("gx", "gy"), pairs)

    def block_z(self, step, turn):
        d = (self.slot - step) % self.holders
        return 2 * d + ((self.item % 2) ^ turn)


class Halving:
    def __init__(self, part, columns=None, wire=BF16):
        self.sizes = {axis: lax.axis_size(axis) for axis in ("gx", "gy")}
        gx, gy = bits_of(self.sizes["gx"]), bits_of(self.sizes["gy"])
        dims = [("gx", b) for b in reversed(range(gx))] + [("gy", b) for b in reversed(range(gy))]
        self.rows = part.shape[0] >> len(dims)
        self.pieces = [([part], dims)]
        rising = [("gx", b) for b in range(1, gx)]
        self.orders = [[("gx", 0)]] + [list(pair) for pair in zip(rising, reversed(rising))]
        self.orders += [[("gy", b)] for b in range(gy)]
        self.columns, self.wire = columns, wire
        if columns is None:
            self.orders = [order[:1] for order in self.orders]

    def cut(self):
        steps = self.orders.pop(0)
        if len(steps) > len(self.pieces):
            (parts, dims), c = self.pieces[0], self.columns
            self.pieces = [([p[:, :c] for p in parts], dims), ([p[:, c:] for p in parts], dims)]
        self.kept, sends = [], []
        together = len(steps) < len(self.pieces)
        for i, (parts, dims) in enumerate(self.pieces):
            axis, bit = steps[0 if together else i]
            place = dims.index((axis, bit))
            before, after = 1 << place, 1 << (len(dims) - place - 1)
            mine = (lax.axis_index(axis) >> bit) & 1

            def half(which):
                total = 0.0
                for p in parts:
                    p = p.reshape((before, 2, after * self.rows) + p.shape[1:])
                    p = lax.dynamic_index_in_dim(p, which, 1, keepdims=False)
                    p = p.reshape((before * after * self.rows,) + p.shape[2:])
                    total = p if len(parts) == 1 else total + p.astype(F32)
                return total.astype(self.wire)

            sends.append(half(1 - mine))
            self.kept.append((half(mine), [d for d in dims if d != (axis, bit)]))
        if together:
            sends = [jnp.concatenate(sends, axis=1)]
            self.kept = [(jnp.concatenate([k for k, _ in self.kept], axis=1), self.kept[0][1])]
        self.steps = steps
        return sends

    def send(self, sends):
        self.pieces = []
        for value, (kept, dims), (axis, bit) in zip(sends, self.kept, self.steps):
            got = lax.ppermute(value, axis, [(i, i ^ (1 << bit)) for i in range(self.sizes[axis])])
            self.pieces.append(([kept, got], dims))

    def advance(self, *others):
        sends = self.cut()
        out = lax.optimization_barrier((*sends, *others))
        self.send(out[: len(sends)])
        return out[len(sends) :] if len(others) != 1 else out[-1]

    def finish(self):
        while self.orders:
            self.send(self.cut())
        (kept, got), _ = self.pieces[0]
        return kept.astype(F32) + got.astype(F32)


LANES = 128
NT = (((1,), (1,)), ((), ()))
TN = (((0,), (0,)), ((), ()))
NN = (((1,), (0,)), ((), ()))
IN_VMEM = pl.BlockSpec(memory_space=pltpu.VMEM)


def dot(left, right, dims):
    return lax.dot_general(left, right, dims, preferred_element_type=F32)


def head_of(ref, head, base=0):
    start = base + head * HEAD_DIM
    return ref[:, start : start + HEAD_DIM].astype(F32)


def widen(value, extras=()):
    rows = value.shape[0]
    out = jnp.concatenate([value, jnp.zeros((rows, LANES - HEAD_DIM), F32)], axis=1)
    lane = lax.broadcasted_iota(jnp.int32, (rows, LANES), 1)
    for i, extra in enumerate(extras):
        out = jnp.where(lane == HEAD_DIM + i, extra, out)
    return out


def thirds(value):
    high = value.astype(BF16).astype(F32)
    rest = value - high
    middle = rest.astype(BF16).astype(F32)
    return high, middle, rest - middle


def attend_kernel(holders, width, chunk, *refs):
    qkv, others, bias, mixed, lse = refs[0], refs[1:holders], refs[holders], *refs[holders + 1 : holders + 3]
    q_s, k_s, v_s, o_s = refs[holders + 3 :]
    rows = qkv.shape[0]
    factor = HEAD_DIM**-0.5 * math.log2(math.e)
    for head in range(HEADS):
        q_s[head] = widen(head_of(qkv, head), (1.0,)).astype(BF16)
        for s in range(holders):
            source, base = (qkv, width) if s == 0 else (others[s - 1], 0)
            part = slice(s * rows, (s + 1) * rows)
            k_s[head, part, :] = widen(head_of(source, head, base), (bias[part, 0:1],)).astype(BF16)
            v_s[head, part, :] = widen(head_of(source, head, base + width), (1.0,)).astype(BF16)
    lane = lax.broadcasted_iota(jnp.int32, (chunk, LANES), 1)

    def one_head(head, carry):
        k, v = k_s[head], v_s[head]
        for r in range(0, rows, chunk):
            scores = dot(q_s[head, r : r + chunk, :], k, NT)
            largest = jnp.max(scores, axis=1, keepdims=True)
            expo = jnp.exp2((scores - largest) * factor).astype(BF16)
            out = dot(expo, v, NN)
            total = out[:, HEAD_DIM : HEAD_DIM + 1]
            o_s[head, r : r + chunk, :] = jnp.where(
                lane == HEAD_DIM, largest * factor + jnp.log2(total), out / total
            )
        return carry

    lax.fori_loop(0, HEADS, one_head, 0)
    lane = lax.broadcasted_iota(jnp.int32, (rows, LANES), 1)
    logs = jnp.zeros((rows, LANES), F32)
    for head in range(HEADS):
        out = o_s[head]
        mixed[:, head * HEAD_DIM : (head + 1) * HEAD_DIM] = out[:, :HEAD_DIM].astype(mixed.dtype)
        logs = jnp.where(lane == head, out[:, HEAD_DIM : HEAD_DIM + 1], logs)
    lse[...] = logs


def attend(qkv, others, bias):
    rows, width, holders = qkv.shape[0], qkv.shape[1] // 3, len(others) + 1
    keys = rows * holders
    return pl.pallas_call(
        partial(attend_kernel, holders, width, 288),
        out_shape=(
            jax.ShapeDtypeStruct((rows, width), BF16),
            jax.ShapeDtypeStruct((rows, LANES), F32),
        ),
        in_specs=[IN_VMEM] * (holders + 1),
        out_specs=(IN_VMEM,) * 2,
        scratch_shapes=[
            pltpu.VMEM((HEADS, rows, LANES), BF16),
            pltpu.VMEM((HEADS, keys, LANES), BF16),
            pltpu.VMEM((HEADS, keys, LANES), BF16),
            pltpu.VMEM((HEADS, rows, LANES), F32),
        ],
        cost_estimate=pl.CostEstimate(
            flops=4 * rows * keys * 512 * HEADS,
            transcendentals=rows * keys * HEADS,
            bytes_accessed=2 * width * (rows * 4 + keys * 2),
        ),
        compiler_params=pltpu.CompilerParams(vmem_limit_bytes=56 << 20),
        name="attend",
    )(qkv, *others, bias)


def attend_back_kernel(holders, width, chunk, first, heads, *refs):
    refs = list(refs)
    qkv, others, bias, mixed, lse, grad = refs[0], refs[1:holders], *refs[holders : holders + 4]
    refs = refs[holders + 4 :]
    last = first + heads == HEADS
    earlier, refs = (refs[:2], refs[2:]) if last and first else ((), refs)
    outs, refs = (refs[: holders + 1], refs[holders + 1 :]) if last else (refs[:2], refs[2:])
    q_s, k_s, v_s, g_s = refs[:4]
    dq_s, dkv_s = refs[4:] if last else outs
    rows = qkv.shape[0]
    keys = rows * holders
    scale = HEAD_DIM**-0.5
    factor = scale * math.log2(math.e)
    for i in range(heads):
        head = first + i
        g = head_of(grad, head)
        delta = jnp.sum(g * head_of(mixed, head), axis=1, keepdims=True)
        shift = thirds(lse[:, head : head + 1] * (-1.0 / factor))
        q_s[i] = widen(head_of(qkv, head), (1.0,) + shift).astype(BF16)
        g_s[i] = widen(g, thirds(-delta)).astype(BF16)
        for s in range(holders):
            source, base = (qkv, width) if s == 0 else (others[s - 1], 0)
            part = slice(s * rows, (s + 1) * rows)
            k = widen(head_of(source, head, base), (bias[part, 0:1], 1.0, 1.0, 1.0))
            k_s[i, part, :] = k.astype(BF16)
            v_s[i, part, :] = widen(head_of(source, head, base + width), (1.0,) * 3).astype(BF16)

    def one_head(i, carry):
        q, g = q_s[i], g_s[i]
        dq = jnp.zeros((LANES, rows), F32)
        for r in range(0, keys, chunk):
            k, v = k_s[i, r : r + chunk, :], v_s[i, r : r + chunk, :]
            probs = jnp.exp2(dot(k, q, NT) * factor)
            ds = (probs * dot(v, g, NT)).astype(BF16)
            dkv_s[0, i, r : r + chunk, :] = (dot(ds, q, NN) * scale).astype(dkv_s.dtype)
            dkv_s[1, i, r : r + chunk, :] = dot(probs.astype(BF16), g, NN).astype(dkv_s.dtype)
            dq = dq + dot(k, ds, TN)
        dq_s[i] = (jnp.transpose(dq) * scale).astype(dq_s.dtype)
        return carry

    lax.fori_loop(0, heads, one_head, 0)
    if not last:
        return
    for head in range(HEADS):
        dq, dkv, i = (dq_s, dkv_s, head - first) if head >= first else (*earlier, head)
        cols = slice(head * HEAD_DIM, (head + 1) * HEAD_DIM)
        outs[0][:, cols] = dq[i][:, :HEAD_DIM].astype(F32).astype(BF16)
        for s in range(holders):
            for which in range(2):
                value = dkv[which, i, s * rows : (s + 1) * rows, :][:, :HEAD_DIM]
                cols = slice(which * width + head * HEAD_DIM, which * width + (head + 1) * HEAD_DIM)
                outs[1 + s][:, cols] = value.astype(F32).astype(BF16)


def attend_back(qkv, others, bias, mixed, lse, grad, first, heads, earlier):
    rows, width, holders = qkv.shape[0], qkv.shape[1] // 3, len(others) + 1
    keys = rows * holders
    last = first + heads == HEADS
    if last:
        out_shape = (jax.ShapeDtypeStruct((rows, width), BF16),) + (
            jax.ShapeDtypeStruct((rows, 2 * width), BF16),
        ) * holders
    else:
        out_shape = (
            jax.ShapeDtypeStruct((heads, rows, LANES), BF16),
            jax.ShapeDtypeStruct((2, heads, keys, LANES), BF16),
        )
    scratch = [
        pltpu.VMEM((heads, rows, LANES), BF16),
        pltpu.VMEM((heads, keys, LANES), BF16),
        pltpu.VMEM((heads, keys, LANES), BF16),
        pltpu.VMEM((heads, rows, LANES), BF16),
    ]
    if last:
        scratch += [
            pltpu.VMEM((heads, rows, LANES), BF16),
            pltpu.VMEM((2, heads, keys, LANES), BF16),
        ]
    return pl.pallas_call(
        partial(attend_back_kernel, holders, width, keys // 2, first, heads),
        out_shape=out_shape,
        in_specs=[IN_VMEM] * (holders + 4 + len(earlier)),
        out_specs=(IN_VMEM,) * len(out_shape),
        scratch_shapes=scratch,
        cost_estimate=pl.CostEstimate(
            flops=10 * rows * keys * 512 * heads,
            transcendentals=rows * keys * heads,
            bytes_accessed=2 * width * (rows * 8 + keys * 4),
        ),
        compiler_params=pltpu.CompilerParams(vmem_limit_bytes=58 << 20),
        name="attend_back",
    )(qkv, *others, bias, mixed, lse, grad, *earlier)


def per_device(
    image_tokens,
    text_tokens,
    image_skip,
    text_skip,
    time_steps,
    caption_len,
    pred_grad,
    text_grad,
    w_skip,
    b_skip,
    gain_attn,
    bias_attn,
    w_qkv,
    w_proj,
    b_proj,
    gain_mlp,
    bias_mlp,
    w_up,
    b_up,
    w_down,
    b_down,
    gain_head,
    bias_head,
    w_head,
    b_head,
    w_conv,
    b_conv,
):
    item_count, text_dev, width = text_tokens.shape
    grid_rows, grid_cols = (image_tokens.shape[1], image_tokens.shape[2])
    image_dev = grid_rows * grid_cols
    assert item_count == 2
    block = -(-(image_dev + text_dev) // 16) * 16
    text_pad = block - image_dev
    rows = 2 * block
    go = Regroup()
    devices = go.gx * go.gy

    lat_shape = pred_grad.shape
    lat_rows, lat_cols = (lat_shape[2], lat_shape[3])
    grad_pad = jnp.pad(with_halo(pred_grad, "gy", 3, 1), ((0, 0), (0, 0), (1, 1), (0, 0)))
    grad_latent = jnp.zeros(lat_shape, F32)
    for row_off in range(3):
        for col_off in range(3):
            grad_latent = grad_latent + jnp.einsum(
                "oi,bohw->bihw",
                w_conv[:, :, row_off, col_off],
                grad_pad[
                    :, :, 2 - row_off : 2 - row_off + lat_rows, 2 - col_off : 2 - col_off + lat_cols
                ],
                precision=HIGHEST,
            )
    grad_patches = jnp.transpose(
        grad_latent.reshape(item_count, LAT_CH, grid_rows, PATCH, grid_cols, PATCH),
        (0, 2, 4, 3, 5, 1),
    ).reshape(item_count, image_dev, LAT_CH * PATCH * PATCH)
    grad_b_head = jnp.sum(grad_patches, axis=(0, 1))
    grad_b_conv = jnp.sum(pred_grad, axis=(0, 2, 3))

    slots = lax.axis_index("gy") * text_dev + jnp.arange(text_dev, dtype=jnp.int32)
    first_row = (slots == 0).astype(F32)
    embed = time_embedding(time_steps, width)
    text_in = (text_tokens.astype(F32) + first_row[None, :, None] * embed[:, None, :]).astype(BF16)

    def rows_of(image, text):
        return jnp.concatenate(
            [
                image.reshape(item_count, image_dev, width),
                jnp.pad(text, ((0, 0), (0, text_pad - text_dev), (0, 0))),
            ],
            axis=1,
        )

    joined_here = jnp.concatenate(
        [rows_of(image_tokens, text_in), rows_of(image_skip, text_skip)], axis=2
    )
    resid_here = (
        project(joined_here.reshape(rows, 2 * width), w_skip) + b_skip
    ).astype(BF16)
    resid = jnp.concatenate(go.there(resid_here.reshape(2, block, width)), axis=0).astype(F32)
    gate, joined_late, text_grad, grad_patches, caption = lax.optimization_barrier(
        (resid, joined_here, text_grad, grad_patches, caption_len.astype(F32))
    )
    resid = gate
    patch_rows = -(-grad_patches.shape[1] * grad_patches.shape[2] // width)
    flat = grad_patches.reshape(2, -1)
    flat = jnp.pad(flat, ((0, 0), (0, patch_rows * width - flat.shape[1])))
    message = jnp.concatenate(
        [
            text_grad,
            flat.reshape(2, patch_rows, width),
            jnp.broadcast_to(caption[:, None, None], (2, 1, width)),
        ],
        axis=1,
    )
    message = go.there(message)
    joined_late, *message = lax.optimization_barrier((joined_late, *message))
    joined = jnp.concatenate(go.there(joined_late), axis=0)
    text_grad_rows = [part[:text_dev] for part in message]
    grad_patches = jnp.concatenate(
        [
            part[text_dev : text_dev + patch_rows].reshape(-1)[: image_dev * 16].reshape(-1, 16)
            for part in message
        ],
        axis=0,
    )
    caption = message[0][-1, 0].astype(jnp.int32)

    normed_attn, attn_norm_back = jax.vjp(layer_norm, resid, gain_attn, bias_attn)
    normed = normed_attn.astype(BF16)
    qkv = project(normed, w_qkv).astype(BF16)
    key_values = qkv[:, width:]
    others = [go.share(key_values, step) for step in range(1, go.holders)]
    inside = jnp.arange(text_pad, dtype=jnp.int32)
    bias = []
    for step in range(go.holders):
        for turn in range(2):
            slot = go.block_z(step, turn) * text_dev + inside
            allowed = (inside < text_dev) & (slot <= caption)
            bias += [jnp.zeros((image_dev,), F32), jnp.where(allowed, 0.0, -1e30)]
    bias = jnp.broadcast_to(jnp.concatenate(bias)[:, None], (rows * go.holders, LANES))
    mixed, lse = attend(qkv, others, bias)

    resid_two = resid + project(mixed, w_proj) + b_proj
    normed_mlp, mlp_norm_back = jax.vjp(layer_norm, resid_two, gain_mlp, bias_mlp)
    normed_two = normed_mlp.astype(BF16)
    pre_act = project(normed_two, w_up) + b_up
    activated, gelu_back = jax.vjp(partial(jax.nn.gelu, approximate=False), pre_act)
    hidden = activated.astype(BF16)
    resid_three = resid_two + project(hidden, w_down) + b_down

    def image_of(values):
        return jnp.concatenate([values[:image_dev], values[block : block + image_dev]], axis=0)

    def text_of(values):
        return [values[image_dev : image_dev + text_dev], values[block + image_dev : block + image_dev + text_dev]]

    text_out = go.back(*[part.astype(BF16) for part in text_of(resid_three)])
    normed_head, head_norm_back = jax.vjp(layer_norm, image_of(resid_three), gain_head, bias_head)
    head_in = normed_head.astype(BF16)
    patches = project(head_in, w_head) + b_head
    patches = go.back(patches[:image_dev], patches[image_dev:])

    patch_grid = patches.reshape(item_count, grid_rows, grid_cols, PATCH, PATCH, LAT_CH)
    latent = jnp.transpose(patch_grid, (0, 5, 1, 3, 2, 4)).reshape(lat_shape)
    padded = jnp.pad(with_halo(latent, "gy", 3, 1), ((0, 0), (0, 0), (1, 1), (0, 0)))
    prediction = jnp.zeros(lat_shape, F32) + b_conv[None, :, None, None]
    conv_taps = []
    for row_off in range(3):
        for col_off in range(3):
            window = padded[:, :, row_off : row_off + lat_rows, col_off : col_off + lat_cols]
            prediction = prediction + jnp.einsum(
                "oi,bihw->bohw", w_conv[:, :, row_off, col_off], window, precision=HIGHEST
            )
            conv_taps.append(jnp.einsum("bohw,bihw->oi", pred_grad, window, precision=HIGHEST))
    grad_w_conv = jnp.stack(conv_taps, axis=-1)

    grad_w_head = jnp.einsum("rd,ro->do", head_in.astype(F32), grad_patches, precision=HIGHEST)
    grad_normed_head = jnp.einsum("ro,do->rd", grad_patches, w_head.astype(F32), precision=HIGHEST)
    grad_image_out, grad_gain_head, grad_bias_head = head_norm_back(grad_normed_head)
    text_padding = ((0, text_pad - text_dev), (0, 0))
    grad_three = jnp.concatenate(
        [
            grad_image_out[:image_dev],
            jnp.pad(text_grad_rows[0], text_padding),
            grad_image_out[image_dev:],
            jnp.pad(text_grad_rows[1], text_padding),
        ],
        axis=0,
    )
    grad_b_down = jnp.sum(grad_three, axis=0)
    down_in = grad_three.astype(BF16)
    sum_down = Halving(weight_grad(hidden, down_in).astype(BF16), 640)
    down_in = sum_down.advance(down_in)
    (grad_pre,) = gelu_back(back_project(down_in, w_down))
    pre_low = grad_pre.astype(BF16)
    grad_b_up = jnp.sum(pre_low.astype(F32), axis=0)
    pre_low = sum_down.advance(pre_low)
    sum_up = Halving(weight_grad(normed_two, pre_low).astype(BF16), 2304)
    pre_low = sum_up.advance(pre_low)
    grad_two, grad_gain_mlp, grad_bias_mlp = mlp_norm_back(back_project(pre_low, w_up))
    grad_two = grad_two + grad_three
    grad_b_proj = jnp.sum(grad_two, axis=0)
    proj_in = grad_two.astype(BF16)
    proj_in = sum_up.advance(proj_in)
    sum_proj = Halving(weight_grad(mixed, proj_in).astype(BF16), 640)
    proj_in = sum_proj.advance(proj_in)
    grad_mixed = back_project(proj_in, w_proj).astype(BF16)
    grad_mixed = sum_down.advance(grad_mixed)
    parts = attend_back(qkv, others, bias, mixed, lse, grad_mixed, 0, HEADS // 2, ())
    parts = sum_proj.advance(*parts)
    parts = sum_up.advance(*parts)
    parts = sum_down.advance(*parts)
    grads = attend_back(qkv, others, bias, mixed, lse, grad_mixed, HEADS // 2, HEADS // 2, parts)
    grads = sum_down.advance(*grads)
    grads = sum_proj.advance(*grads)
    grads = sum_up.advance(*grads)
    grad_kv = grads[1].astype(F32)
    for step in range(1, go.holders):
        grad_kv = grad_kv + go.share(grads[1 + step], go.holders - step).astype(F32)
    grad_qkv = jnp.concatenate([grads[0], grad_kv.astype(BF16)], axis=1)
    sum_qkv = Halving(weight_grad(normed, grad_qkv).astype(BF16), 1792)
    grad_qkv = sum_qkv.advance(grad_qkv)
    grad_one, grad_gain_attn, grad_bias_attn = attn_norm_back(back_project(grad_qkv, w_qkv))
    grad_one = grad_one + grad_two
    grad_b_skip = jnp.sum(grad_one, axis=0)
    skip_in = grad_one.astype(BF16)
    skip_in = sum_qkv.advance(skip_in)
    sum_skip = Halving(weight_grad(joined, skip_in).astype(BF16), 640)
    skip_in = sum_skip.advance(skip_in)
    skip_here = go.back(skip_in[:block], skip_in[block:])
    grad_joined = back_project(skip_here.reshape(rows, width), w_skip).reshape(2, block, 2 * width)
    image_shape = image_tokens.shape
    grad_image = grad_joined[:, :image_dev, :width].reshape(image_shape)
    grad_image_skip = grad_joined[:, :image_dev, width:].reshape(image_shape)
    grad_text = grad_joined[:, image_dev : image_dev + text_dev, :width]
    grad_text_skip = grad_joined[:, image_dev : image_dev + text_dev, width:]

    vectors = (
        grad_b_skip,
        grad_gain_attn,
        grad_bias_attn,
        grad_b_proj,
        grad_gain_mlp,
        grad_bias_mlp,
        grad_b_up,
        grad_b_down,
        grad_gain_head,
        grad_bias_head,
        grad_w_head,
    )
    whole = jnp.concatenate([grad_b_head, grad_w_conv.reshape(-1), grad_b_conv])
    packed = [v.reshape(devices, -1) for v in vectors]
    packed.append(jnp.broadcast_to(whole[None], (devices, whole.shape[0])))
    packed = jnp.concatenate(packed, axis=1)
    packed = jnp.pad(packed, ((0, 0), (0, -packed.shape[1] % 128)))
    packed = Halving(packed, None, F32).finish()[0]
    small = []
    start = 0
    for v in vectors:
        size = v.size // devices
        small.append(packed[start : start + size])
        start += size
    small[-1] = small[-1].reshape(-1, grad_w_head.shape[1])
    whole = packed[start : start + whole.shape[0]]
    patch_size = grad_b_head.shape[0]
    taps = grad_w_conv.size
    return (
        prediction,
        text_out,
        grad_image,
        grad_text,
        grad_image_skip,
        grad_text_skip,
        sum_skip.finish(),
        small[0],
        small[1],
        small[2],
        sum_qkv.finish(),
        sum_proj.finish(),
        small[3],
        small[4],
        small[5],
        sum_up.finish(),
        small[6],
        sum_down.finish(),
        small[7],
        small[8],
        small[9],
        small[10],
        whole[:patch_size],
        whole[patch_size : patch_size + taps].reshape(LAT_CH, LAT_CH, 3, 3),
        whole[patch_size + taps :],
    )


def solution(mesh):
    rows = P(("gx", "gy"))
    image = P("gx", None, "gy", None)
    text = P("gx", "gy", None)
    latent = P("gx", None, None, "gy")
    return jax.shard_map(
        per_device,
        mesh=mesh,
        in_specs=(image, text, image, text, P("gx"), P("gx"), latent, text) + (P(),) * 19,
        out_specs=(latent, text, image, text, image, text) + (rows,) * 16 + (P(),) * 3,
        check_vma=False,
    )
```

```python
from functools import partial
import math

import jax
import jax.numpy as jnp
from jax import lax
from jax.experimental import pallas as pl
from jax.experimental.pallas import tpu as pltpu
from jax.sharding import PartitionSpec as P

HEADS = 16
HEAD_DIM = 72
LAT_CH = 4
PATCH = 2
LANES = 128
NT = (((1,), (1,)), ((), ()))
TN = (((0,), (0,)), ((), ()))
NN = (((1,), (0,)), ((), ()))

EPSILON = 1e-05
HIGHEST = lax.Precision.HIGHEST
F32 = jnp.float32
BF16 = jnp.bfloat16
COVER = pl.CostEstimate(flops=1 << 20, transcendentals=0, bytes_accessed=1 << 20)


def bits_of(count):
    bits = count.bit_length() - 1
    assert 1 << bits == count
    return bits


def with_halo(block, axis, dim, width):
    count = lax.axis_size(axis)
    forward = [(i, i + 1) for i in range(count - 1)]
    backward = [(target, source) for source, target in forward]
    low = lax.ppermute(
        lax.slice_in_dim(block, block.shape[dim] - width, None, axis=dim), axis, forward
    )
    high = lax.ppermute(lax.slice_in_dim(block, 0, width, axis=dim), axis, backward)
    return jnp.concatenate([low, block, high], axis=dim)


def layer_norm(values, gain, bias):
    centre = jnp.mean(values, axis=-1, keepdims=True)
    centred = values - centre
    variance = jnp.mean(centred * centred, axis=-1, keepdims=True)
    return centred * lax.rsqrt(variance + EPSILON) * gain + bias


def time_embedding(time_steps, model_width):
    half_width = model_width // 2
    freqs = jnp.exp(-math.log(10000.0) * jnp.arange(half_width, dtype=F32) / half_width)
    angles = time_steps.astype(F32)[:, None] * freqs[None, :]
    return jnp.concatenate([jnp.cos(angles), jnp.sin(angles)], axis=1)


ERFC = (
    -1.26551223,
    1.00002368,
    0.37409196,
    0.09678418,
    -0.18628806,
    0.27886807,
    -1.13520398,
    1.48851587,
    -0.82215223,
    0.17087277,
)


def gelu_and_slope(values):
    u = jnp.abs(values) * math.sqrt(0.5)
    t = 1.0 / (1.0 + 0.5 * u)
    poly = jnp.full_like(t, ERFC[-1])
    for coefficient in reversed(ERFC[:-1]):
        poly = poly * t + coefficient
    bell = jnp.exp(-u * u)
    tail = 0.5 * t * bell * jnp.exp(poly)
    below = jnp.where(values < 0.0, tail, 1.0 - tail)
    return values * below, below + values * bell * (1.0 / math.sqrt(2.0 * math.pi))


def project(rows, weight):
    return jnp.einsum("rd,de->re", rows, weight, preferred_element_type=F32)


def back_project(grads, weight):
    return jnp.einsum("re,de->rd", grads, weight, preferred_element_type=F32)


class Regroup:
    def __init__(self):
        self.gx, self.gy = lax.axis_size("gx"), lax.axis_size("gy")
        self.ratio = self.gy // 4
        assert self.ratio * 4 == self.gy and self.gx % 2 == 0
        core, z = lax.axis_index("gx") % 2, lax.axis_index("gy")
        self.parity = z % 2
        self.item = z // self.ratio
        self.slot = (z % self.ratio) * 2 + core
        self.holders = 2 * self.ratio
        self.perms = []
        for turn in range(2):
            pairs = []
            for gx in range(self.gx):
                pair, c = gx // 2, gx % 2
                for z in range(self.gy):
                    f = (z & 1) ^ turn
                    item, d = 2 * c + f, z // 2
                    to_z, to_c = item * self.ratio + d // 2, d % 2
                    pairs.append((gx * self.gy + z, (2 * pair + to_c) * self.gy + to_z))
            self.perms.append(pairs)

    def cut(self, blocks):
        return [
            lax.dynamic_index_in_dim(blocks, self.parity ^ turn, 0, keepdims=False)
            for turn in range(2)
        ]

    def send(self, sends):
        return [lax.ppermute(sends[t], ("gx", "gy"), self.perms[t]) for t in range(2)]

    def there(self, blocks):
        return self.send(self.cut(blocks))

    def back(self, first, second):
        got = [
            lax.ppermute(part, ("gx", "gy"), [(b, a) for a, b in self.perms[turn]])
            for turn, part in enumerate((first, second))
        ]
        even = self.parity == 0
        return jnp.stack([jnp.where(even, got[0], got[1]), jnp.where(even, got[1], got[0])])

    def share(self, rows, step):
        pairs = []
        for gx in range(self.gx):
            pair, c = gx // 2, gx % 2
            for z in range(self.gy):
                base, d = z // self.ratio * self.ratio, (z % self.ratio) * 2 + c
                to = (d + step) % self.holders
                pairs.append(
                    (gx * self.gy + z, (2 * pair + to % 2) * self.gy + base + to // 2)
                )
        return lax.ppermute(rows, ("gx", "gy"), pairs)

    def block_z(self, step, turn):
        d = (self.slot - step) % self.holders
        return 2 * d + ((self.item % 2) ^ turn)


def back_kernel(grads, weight, *refs):
    value = dot(grads[...], weight[...], NT)
    if len(refs) == 2:
        value = value * refs[0][...].astype(F32)
    refs[-1][...] = value.astype(refs[-1].dtype)


def back(grads, weight, dtype, *slope):
    count, width = grads.shape
    height = weight.shape[0]
    tile = 1152 if width == 1152 and height % 1152 == 0 else 384
    tile = tile if height % tile == 0 else height
    part = pl.BlockSpec((count, tile), lambda j: (0, j))
    return pl.pallas_call(
        back_kernel,
        out_shape=jax.ShapeDtypeStruct((count, height), dtype),
        grid=(height // tile,),
        in_specs=[
            pl.BlockSpec((count, width), lambda j: (0, 0)),
            pl.BlockSpec((tile, width), lambda j: (j, 0)),
            *[part for _ in slope],
        ],
        out_specs=part,
        compiler_params=pltpu.CompilerParams(vmem_limit_bytes=48 << 20),
        cost_estimate=COVER,
        name="back",
    )(grads, weight, *slope)


def weight_grad_kernel(pairs, block, other, rows, grads, full, send, sums):
    full[...] = dot(rows[...], grads[...], TN).astype(full.dtype)
    for pair in range(pairs):
        start = pl.multiple_of((2 * pair + other[0]) * block, 16)
        send[pair * block : (pair + 1) * block, :] = full[pl.ds(start, block), :]
    sums[...] = jnp.sum(grads[...].astype(F32), axis=0, keepdims=True)


def weight_grad(rows, grads):
    count, height = rows.shape
    width = grads.shape[1]
    block = height >> bits_of(lax.axis_size("gx"))
    tall = 1152 if height % 1152 == 0 and 1152 % (2 * block) == 0 else height
    wide = 1152 if width % 1152 == 0 else width
    other = (1 - lax.axis_index("gx") % 2).astype(jnp.int32).reshape(1)
    return pl.pallas_call(
        partial(weight_grad_kernel, tall // (2 * block), block),
        out_shape=(
            jax.ShapeDtypeStruct((height, width), BF16),
            jax.ShapeDtypeStruct((height // 2, width), BF16),
            jax.ShapeDtypeStruct((1, width), F32),
        ),
        grid_spec=pltpu.PrefetchScalarGridSpec(
            num_scalar_prefetch=1,
            grid=(height // tall, width // wide),
            in_specs=[
                pl.BlockSpec((count, tall), lambda i, j, ref: (0, i)),
                pl.BlockSpec((count, wide), lambda i, j, ref: (0, j)),
            ],
            out_specs=[
                pl.BlockSpec((tall, wide), lambda i, j, ref: (i, j)),
                pl.BlockSpec((tall // 2, wide), lambda i, j, ref: (i, j)),
                pl.BlockSpec((1, wide), lambda i, j, ref: (0, j)),
            ],
        ),
        compiler_params=pltpu.CompilerParams(vmem_limit_bytes=48 << 20),
        cost_estimate=COVER,
        name="weight_grad",
    )(other, rows, grads)


def split_kernel(count, places, rows, index, *refs):
    parts, outs, acc = refs[:count], refs[count : count + places], refs[-1]
    value = parts[0][...].astype(F32)
    for part in parts[1:]:
        value = value + part[...].astype(F32)
    acc[...] = value
    z = index[index.shape[0] - 1]
    for place in range(places):

        @pl.when(z == place)
        def _():
            for step in range(places):
                start = (place + step) % places * rows
                outs[step][...] = acc[start : start + rows, :].astype(outs[step].dtype)


def split(addends, index, places, wire):
    block, width = addends[0][0].shape[-2:]
    rows = block // places
    tile = 1152 if width % 1152 == 0 else width

    def spec(dims):
        return pl.BlockSpec(
            (None,) * len(dims) + (block, tile), lambda j, ref: (*[ref[d] for d in dims], 0, j)
        )

    return pl.pallas_call(
        partial(split_kernel, len(addends), places, rows),
        out_shape=[
            jax.ShapeDtypeStruct((rows, width), wire if step else F32) for step in range(places)
        ],
        grid_spec=pltpu.PrefetchScalarGridSpec(
            num_scalar_prefetch=1,
            grid=(width // tile,),
            in_specs=[spec(dims) for _, dims in addends],
            out_specs=[pl.BlockSpec((rows, tile), lambda j, ref: (0, j))] * places,
            scratch_shapes=[pltpu.VMEM((block, tile), F32)],
        ),
        compiler_params=pltpu.CompilerParams(vmem_limit_bytes=40 << 20),
        name="split",
    )(index, *[value for value, _ in addends])


class Scatter:
    def __init__(self, line, part, falling, wire=BF16, first=None):
        self.gx, self.gy = lax.axis_size("gx"), lax.axis_size("gy")
        bits = bits_of(self.gx)
        rest = range(1, bits)
        self.stages = [0] + list(reversed(rest) if falling else rest) + [None]
        block = part.shape[0] >> bits
        dims = list(reversed(range(bits)))
        self.addends = [(part.reshape((2,) * bits + (block, part.shape[1])), dims)]
        self.fixed, self.first = {}, first
        self.line, self.wire = line, wire

    def mine(self, bit):
        return (lax.axis_index("gx") >> bit) & 1

    def total(self, chosen):
        out = None
        for value, dims in self.addends:
            tail = value.shape[len(dims) :]
            starts = [chosen.get(d, 0) for d in dims] + [0] * len(tail)
            shape = tuple(1 if d in chosen else 2 for d in dims) + tail
            value = lax.dynamic_slice(value, [jnp.int32(i) for i in starts], shape)
            value = value.reshape(tuple(2 for d in dims if d not in chosen) + tail)
            out = value if out is None else out.astype(F32) + value.astype(F32)
        return out

    def cut(self, after):
        bit = self.bit = self.stages.pop(0)
        if bit == 0 and self.first is not None:
            return [self.first]
        newest, dims = self.addends[-1]
        newest = lax.optimization_barrier((newest, *after, *self.line))[0]
        self.addends[-1] = (newest, dims)
        if bit is not None:
            send = self.total({**self.fixed, bit: 1 - self.mine(bit)}).astype(self.wire)
            return [send.reshape(-1, send.shape[-1])]
        z = lax.axis_index("gy")
        block, width = self.addends[0][0].shape[-2:]
        rows = block // self.gy
        if rows % 8:
            bits = bits_of(self.gx)
            index = jnp.stack([self.mine(d) for d in range(bits)] + [z]).astype(jnp.int32)
            self.keep, *sends = split(self.addends, index, self.gy, self.wire)
            return sends
        shares = []
        whole = self.addends
        for step in range(self.gy):
            place = lax.rem(z + step, self.gy)
            self.addends = [
                (value.reshape(value.shape[:-2] + (self.gy, rows, width)), dims) for value, dims in whole
            ]
            out = None
            for value, dims in self.addends:
                starts = [jnp.int32(self.fixed[d]) for d in dims] + [place, 0, 0]
                value = lax.dynamic_slice(
                    value, [jnp.int32(i) for i in starts], (1,) * (len(dims) + 1) + (rows, width)
                ).reshape(rows, width)
                out = value if out is None else out.astype(F32) + value.astype(F32)
            shares.append(out.astype(self.wire) if step else out.astype(F32))
        self.keep, *sends = shares
        return sends

    def send(self, sends):
        if self.bit is None:
            self.got = [
                lax.ppermute(value, "gy", [(i, (i + step) % self.gy) for i in range(self.gy)])
                for step, value in enumerate(sends, 1)
            ]
            return
        bit = self.bit
        pairs = [(i, i ^ (1 << bit)) for i in range(self.gx)]
        got = lax.ppermute(sends[0], "gx", pairs)
        dims = [d for d in reversed(range(bits_of(self.gx))) if d not in self.fixed and d != bit]
        tail = self.addends[0][0].shape[-2:]
        self.addends.append((got.reshape((2,) * len(dims) + tail), dims))
        self.fixed[bit] = self.mine(bit)

    def advance(self, *others, after=()):
        sends = self.cut(after)
        count = len(sends)
        out = lax.optimization_barrier((*sends, *others))
        self.send(out[:count])
        self.line[:] = [out[count - 1]]
        return out[count:] if len(others) != 1 else out[-1]

    def finish(self):
        while self.stages:
            self.advance()
        out = self.keep
        for got in lax.optimization_barrier((*self.got, *self.line))[: len(self.got)]:
            out = out + got.astype(F32)
        return out


IN_VMEM = pl.BlockSpec(memory_space=pltpu.VMEM)


def dot(left, right, dims):
    return lax.dot_general(left, right, dims, preferred_element_type=F32)


def head_of(ref, head, base=0):
    start = base + head * HEAD_DIM
    return ref[:, start : start + HEAD_DIM].astype(F32)


def widen(value, extras=()):
    rows = value.shape[0]
    out = jnp.concatenate([value, jnp.zeros((rows, LANES - HEAD_DIM), F32)], axis=1)
    lane = lax.broadcasted_iota(jnp.int32, (rows, LANES), 1)
    for i, extra in enumerate(extras):
        out = jnp.where(lane == HEAD_DIM + i, extra, out)
    return out


def thirds(value):
    high = value.astype(BF16).astype(F32)
    rest = value - high
    middle = rest.astype(BF16).astype(F32)
    return high, middle, rest - middle


def attend_kernel(holders, width, chunk, *refs):
    qkv, others, bias, mixed, lse = refs[0], refs[1:holders], refs[holders], *refs[holders + 1 : holders + 3]
    q_s, k_s, v_s, o_s = refs[holders + 3 :]
    rows = qkv.shape[0]
    factor = HEAD_DIM**-0.5 * math.log2(math.e)
    for head in range(HEADS):
        q_s[head] = widen(head_of(qkv, head), (1.0,)).astype(BF16)
        for s in range(holders):
            source, base = (qkv, width) if s == 0 else (others[s - 1], 0)
            part = slice(s * rows, (s + 1) * rows)
            k_s[head, part, :] = widen(head_of(source, head, base), (bias[part, 0:1],)).astype(BF16)
            v_s[head, part, :] = widen(head_of(source, head, base + width), (1.0,)).astype(BF16)
    lane = lax.broadcasted_iota(jnp.int32, (chunk, LANES), 1)

    def one_head(head, carry):
        k, v = k_s[head], v_s[head]
        for r in range(0, rows, chunk):
            scores = dot(q_s[head, r : r + chunk, :], k, NT)
            largest = jnp.max(scores, axis=1, keepdims=True)
            expo = jnp.exp2((scores - largest) * factor).astype(BF16)
            out = dot(expo, v, NN)
            total = out[:, HEAD_DIM : HEAD_DIM + 1]
            o_s[head, r : r + chunk, :] = jnp.where(
                lane == HEAD_DIM, largest * factor + jnp.log2(total), out / total
            )
        return carry

    lax.fori_loop(0, HEADS, one_head, 0)
    lane = lax.broadcasted_iota(jnp.int32, (rows, LANES), 1)
    logs = jnp.zeros((rows, LANES), F32)
    for head in range(HEADS):
        out = o_s[head]
        mixed[:, head * HEAD_DIM : (head + 1) * HEAD_DIM] = out[:, :HEAD_DIM].astype(mixed.dtype)
        logs = jnp.where(lane == head, out[:, HEAD_DIM : HEAD_DIM + 1], logs)
    lse[...] = logs


def attend(qkv, others, bias):
    rows, width, holders = qkv.shape[0], qkv.shape[1] // 3, len(others) + 1
    keys = rows * holders
    return pl.pallas_call(
        partial(attend_kernel, holders, width, 288),
        out_shape=(
            jax.ShapeDtypeStruct((rows, width), BF16),
            jax.ShapeDtypeStruct((rows, LANES), F32),
        ),
        in_specs=[IN_VMEM] * (holders + 1),
        out_specs=(IN_VMEM,) * 2,
        scratch_shapes=[
            pltpu.VMEM((HEADS, rows, LANES), BF16),
            pltpu.VMEM((HEADS, keys, LANES), BF16),
            pltpu.VMEM((HEADS, keys, LANES), BF16),
            pltpu.VMEM((HEADS, rows, LANES), F32),
        ],
        cost_estimate=COVER,
        compiler_params=pltpu.CompilerParams(vmem_limit_bytes=56 << 20),
        name="attend",
    )(qkv, *others, bias)


def attend_back_kernel(holders, width, chunk, first, heads, *refs):
    refs = list(refs)
    qkv, others, bias, mixed, lse, grad = refs[0], refs[1:holders], *refs[holders : holders + 4]
    refs = refs[holders + 4 :]
    last = first + heads == HEADS
    earlier, refs = (refs[:2], refs[2:]) if last and first else ((), refs)
    outs, refs = (refs[: holders + 1], refs[holders + 1 :]) if last else (refs[:2], refs[2:])
    q_s, k_s, v_s, g_s = refs[:4]
    dq_s, dkv_s = refs[4:] if last else outs
    rows = qkv.shape[0]
    keys = rows * holders
    scale = HEAD_DIM**-0.5
    factor = scale * math.log2(math.e)
    for i in range(heads):
        head = first + i
        g = head_of(grad, head)
        delta = jnp.sum(g * head_of(mixed, head), axis=1, keepdims=True)
        shift = thirds(lse[:, head : head + 1] * (-1.0 / factor))
        q_s[i] = widen(head_of(qkv, head), (1.0,) + shift).astype(BF16)
        g_s[i] = widen(g, thirds(-delta)).astype(BF16)
        for s in range(holders):
            source, base = (qkv, width) if s == 0 else (others[s - 1], 0)
            part = slice(s * rows, (s + 1) * rows)
            k = widen(head_of(source, head, base), (bias[part, 0:1], 1.0, 1.0, 1.0))
            k_s[i, part, :] = k.astype(BF16)
            v_s[i, part, :] = widen(head_of(source, head, base + width), (1.0,) * 3).astype(BF16)

    def one_head(i, carry):
        q, g = q_s[i], g_s[i]
        dq = jnp.zeros((LANES, rows), F32)
        for r in range(0, keys, chunk):
            k, v = k_s[i, r : r + chunk, :], v_s[i, r : r + chunk, :]
            probs = jnp.exp2(dot(k, q, NT) * factor)
            ds = (probs * dot(v, g, NT)).astype(BF16)
            dkv_s[0, i, r : r + chunk, :] = (dot(ds, q, NN) * scale).astype(dkv_s.dtype)
            dkv_s[1, i, r : r + chunk, :] = dot(probs.astype(BF16), g, NN).astype(dkv_s.dtype)
            dq = dq + dot(k, ds, TN)
        dq_s[i] = (jnp.transpose(dq) * scale).astype(dq_s.dtype)
        return carry

    lax.fori_loop(0, heads, one_head, 0)
    if not last:
        return
    for head in range(HEADS):
        dq, dkv, i = (dq_s, dkv_s, head - first) if head >= first else (*earlier, head)
        cols = slice(head * HEAD_DIM, (head + 1) * HEAD_DIM)
        outs[0][:, cols] = dq[i][:, :HEAD_DIM].astype(F32).astype(BF16)
        for s in range(holders):
            for which in range(2):
                value = dkv[which, i, s * rows : (s + 1) * rows, :][:, :HEAD_DIM]
                cols = slice(which * width + head * HEAD_DIM, which * width + (head + 1) * HEAD_DIM)
                outs[1 + s][:, cols] = value.astype(F32).astype(BF16)


def attend_back(qkv, others, bias, mixed, lse, grad, first, heads, earlier):
    rows, width, holders = qkv.shape[0], qkv.shape[1] // 3, len(others) + 1
    keys = rows * holders
    last = first + heads == HEADS
    if last:
        out_shape = (jax.ShapeDtypeStruct((rows, width), BF16),) + (
            jax.ShapeDtypeStruct((rows, 2 * width), BF16),
        ) * holders
    else:
        out_shape = (
            jax.ShapeDtypeStruct((heads, rows, LANES), BF16),
            jax.ShapeDtypeStruct((2, heads, keys, LANES), BF16),
        )
    scratch = [
        pltpu.VMEM((heads, rows, LANES), BF16),
        pltpu.VMEM((heads, keys, LANES), BF16),
        pltpu.VMEM((heads, keys, LANES), BF16),
        pltpu.VMEM((heads, rows, LANES), BF16),
    ]
    if last:
        scratch += [
            pltpu.VMEM((heads, rows, LANES), BF16),
            pltpu.VMEM((2, heads, keys, LANES), BF16),
        ]
    return pl.pallas_call(
        partial(attend_back_kernel, holders, width, keys // 2, first, heads),
        out_shape=out_shape,
        in_specs=[IN_VMEM] * (holders + 4 + len(earlier)),
        out_specs=(IN_VMEM,) * len(out_shape),
        scratch_shapes=scratch,
        cost_estimate=COVER,
        compiler_params=pltpu.CompilerParams(vmem_limit_bytes=58 << 20),
        name="attend_back",
    )(qkv, *others, bias, mixed, lse, grad, *earlier)


def per_device(
    image_tokens,
    text_tokens,
    image_skip,
    text_skip,
    time_steps,
    caption_len,
    pred_grad,
    text_grad,
    w_skip,
    b_skip,
    gain_attn,
    bias_attn,
    w_qkv,
    w_proj,
    b_proj,
    gain_mlp,
    bias_mlp,
    w_up,
    b_up,
    w_down,
    b_down,
    gain_head,
    bias_head,
    w_head,
    b_head,
    w_conv,
    b_conv,
):
    item_count, text_dev, width = text_tokens.shape
    grid_rows, grid_cols = (image_tokens.shape[1], image_tokens.shape[2])
    image_dev = grid_rows * grid_cols
    assert item_count == 2
    block = -(-(image_dev + text_dev) // 16) * 16
    text_pad = block - image_dev
    rows = 2 * block
    go = Regroup()
    devices = go.gx * go.gy

    caption = jnp.broadcast_to(caption_len.astype(F32)[:, None, None], (2, 1, width))
    message = go.there(jnp.concatenate([text_grad, caption], axis=1))

    slots = lax.axis_index("gy") * text_dev + jnp.arange(text_dev, dtype=jnp.int32)
    first_row = (slots == 0).astype(F32)
    embed = time_embedding(time_steps, width)
    text_in = (text_tokens.astype(F32) + first_row[None, :, None] * embed[:, None, :]).astype(BF16)

    def rows_of(image, text):
        return jnp.concatenate(
            [
                image.reshape(item_count, image_dev, width),
                jnp.pad(text, ((0, 0), (0, text_pad - text_dev), (0, 0))),
            ],
            axis=1,
        )

    joined_here = jnp.concatenate(
        [rows_of(image_tokens, text_in), rows_of(image_skip, text_skip)], axis=2
    )
    resid_here = (
        project(joined_here.reshape(rows, 2 * width), w_skip) + b_skip
    ).astype(BF16)
    away = go.cut(resid_here.reshape(2, block, width))
    *away, pred_grad = lax.optimization_barrier((*away, pred_grad))
    lat_shape = pred_grad.shape
    lat_rows, lat_cols = (lat_shape[2], lat_shape[3])
    grad_pad = jnp.pad(with_halo(pred_grad, "gy", 3, 1), ((0, 0), (0, 0), (1, 1), (0, 0)))
    grad_latent = jnp.zeros(lat_shape, F32)
    for row_off in range(3):
        for col_off in range(3):
            grad_latent = grad_latent + jnp.einsum(
                "oi,bohw->bihw",
                w_conv[:, :, row_off, col_off],
                grad_pad[
                    :, :, 2 - row_off : 2 - row_off + lat_rows, 2 - col_off : 2 - col_off + lat_cols
                ],
                precision=HIGHEST,
            )
    grad_patches = jnp.transpose(
        grad_latent.reshape(item_count, LAT_CH, grid_rows, PATCH, grid_cols, PATCH),
        (0, 2, 4, 3, 5, 1),
    ).reshape(item_count, image_dev, LAT_CH * PATCH * PATCH)
    grad_b_head = jnp.sum(grad_patches, axis=(0, 1))
    grad_b_conv = jnp.sum(pred_grad, axis=(0, 2, 3))

    resid = jnp.concatenate(go.send(away), axis=0).astype(F32)
    resid, joined_late, grad_patches = lax.optimization_barrier((resid, joined_here, grad_patches))
    joined = go.there(joined_late)
    patch_rows = -(-grad_patches.shape[1] * grad_patches.shape[2] // LANES)
    flat = grad_patches.reshape(2, -1)
    flat = jnp.pad(flat, ((0, 0), (0, patch_rows * LANES - flat.shape[1])))
    grad_patches = jnp.concatenate(
        [
            part.reshape(-1)[: image_dev * 16].reshape(-1, 16)
            for part in go.there(flat.reshape(2, patch_rows, LANES))
        ],
        axis=0,
    )
    text_grad_rows = [part[:text_dev] for part in message]
    caption = message[0][-1, 0].astype(jnp.int32)

    normed_attn, attn_norm_back = jax.vjp(layer_norm, resid, gain_attn, bias_attn)
    normed = normed_attn.astype(BF16)
    qkv = project(normed, w_qkv).astype(BF16)
    key_values = qkv[:, width:]
    others = [go.share(key_values, step) for step in range(1, go.holders)]
    inside = jnp.arange(text_pad, dtype=jnp.int32)
    bias = []
    for step in range(go.holders):
        for turn in range(2):
            slot = go.block_z(step, turn) * text_dev + inside
            allowed = (inside < text_dev) & (slot <= caption)
            bias += [jnp.zeros((image_dev,), F32), jnp.where(allowed, 0.0, -1e30)]
    bias = jnp.broadcast_to(jnp.concatenate(bias)[:, None], (rows * go.holders, LANES))
    mixed, lse = attend(qkv, others, bias)

    resid_two = resid + project(mixed, w_proj) + b_proj
    normed_mlp, mlp_norm_back = jax.vjp(layer_norm, resid_two, gain_mlp, bias_mlp)
    normed_two = normed_mlp.astype(BF16)
    pre_act = project(normed_two, w_up) + b_up
    activated, slope = gelu_and_slope(pre_act)
    hidden, slope = activated.astype(BF16), slope.astype(BF16)
    hidden, slope, *joined = lax.optimization_barrier((hidden, slope, *joined))
    joined = jnp.concatenate(joined, axis=0)
    resid_three = resid_two + project(hidden, w_down) + b_down

    def image_of(values):
        return jnp.concatenate([values[:image_dev], values[block : block + image_dev]], axis=0)

    def text_of(values):
        return [values[image_dev : image_dev + text_dev], values[block + image_dev : block + image_dev + text_dev]]

    text_out = go.back(*[part.astype(BF16) for part in text_of(resid_three)])
    normed_head, head_norm_back = jax.vjp(layer_norm, image_of(resid_three), gain_head, bias_head)
    head_in = normed_head.astype(BF16)
    patches = project(head_in, w_head) + b_head
    patches = go.back(patches[:image_dev], patches[image_dev:])

    patch_grid = patches.reshape(item_count, grid_rows, grid_cols, PATCH, PATCH, LAT_CH)
    latent = jnp.transpose(patch_grid, (0, 5, 1, 3, 2, 4)).reshape(lat_shape)
    padded = jnp.pad(with_halo(latent, "gy", 3, 1), ((0, 0), (0, 0), (1, 1), (0, 0)))
    prediction = jnp.zeros(lat_shape, F32) + b_conv[None, :, None, None]
    conv_taps = []
    for row_off in range(3):
        for col_off in range(3):
            window = padded[:, :, row_off : row_off + lat_rows, col_off : col_off + lat_cols]
            prediction = prediction + jnp.einsum(
                "oi,bihw->bohw", w_conv[:, :, row_off, col_off], window, precision=HIGHEST
            )
            conv_taps.append(jnp.einsum("bohw,bihw->oi", pred_grad, window, precision=HIGHEST))
    grad_w_conv = jnp.stack(conv_taps, axis=-1)

    grad_w_head = jnp.einsum("rd,ro->do", head_in.astype(F32), grad_patches, precision=HIGHEST)
    grad_normed_head = jnp.einsum("ro,do->rd", grad_patches, w_head.astype(F32), precision=HIGHEST)
    grad_image_out, grad_gain_head, grad_bias_head = head_norm_back(grad_normed_head)
    text_padding = ((0, text_pad - text_dev), (0, 0))
    grad_three = jnp.concatenate(
        [
            grad_image_out[:image_dev],
            jnp.pad(text_grad_rows[0], text_padding),
            grad_image_out[image_dev:],
            jnp.pad(text_grad_rows[1], text_padding),
        ],
        axis=0,
    )
    grad_b_down = jnp.sum(grad_three, axis=0)
    line = []

    def scatter(left, right, falling):
        full, first, sums = weight_grad(left, right)
        return Scatter(line, full, falling, BF16, first), sums[0]

    down_in = grad_three.astype(BF16)
    sum_down, _ = scatter(hidden, down_in, False)
    down_in = sum_down.advance(down_in)
    pre_low = back(down_in, w_down, BF16, slope)
    pre_low = sum_down.advance(pre_low)
    sum_up, grad_b_up = scatter(normed_two, pre_low, True)
    pre_low = sum_up.advance(pre_low)
    grad_two, grad_gain_mlp, grad_bias_mlp = mlp_norm_back(back(pre_low, w_up, F32))
    grad_two = grad_two + grad_three
    grad_b_proj = jnp.sum(grad_two, axis=0)
    proj_in = grad_two.astype(BF16)
    proj_in = sum_up.advance(proj_in)
    sum_proj, _ = scatter(mixed, proj_in, False)
    proj_in = sum_proj.advance(proj_in)
    grad_mixed = back(proj_in, w_proj, BF16)
    parts = attend_back(qkv, others, bias, mixed, lse, grad_mixed, 0, HEADS // 2, ())
    parts = sum_proj.advance(*parts, after=parts[:1])
    parts = sum_down.advance(*parts)
    grads = attend_back(qkv, others, bias, mixed, lse, grad_mixed, HEADS // 2, HEADS // 2, parts)
    shared = [go.share(grads[1 + step], go.holders - step) for step in range(1, go.holders)]
    sum_q, _ = scatter(normed, grads[0], True)
    first = sum_q.advance(grads[1])
    first = sum_up.advance(first, after=grads[:1])
    grad_kv = first.astype(F32)
    for value in shared:
        grad_kv = grad_kv + value.astype(F32)
    grad_kv = grad_kv.astype(BF16)
    sum_kv, _ = scatter(normed, grad_kv, False)
    grad_kv = sum_kv.advance(grad_kv)
    grad_kv = sum_proj.advance(grad_kv)
    grad_kv = sum_down.advance(grad_kv)
    grad_kv = sum_q.advance(grad_kv)
    grad_qkv = jnp.concatenate([grads[0], grad_kv], axis=1)
    grad_one = back(grad_qkv, w_qkv, F32)
    grad_one = sum_kv.advance(grad_one, after=(grad_one,))
    grad_one, grad_gain_attn, grad_bias_attn = attn_norm_back(grad_one)
    grad_one = grad_one + grad_two
    grad_b_skip = jnp.sum(grad_one, axis=0)
    skip_in = grad_one.astype(BF16)
    skip_here = go.back(skip_in[:block], skip_in[block:])
    sum_skip, _ = scatter(joined, skip_in, True)
    sum_skip.advance()
    vectors = (
        grad_b_skip,
        grad_gain_attn,
        grad_bias_attn,
        grad_b_proj,
        grad_gain_mlp,
        grad_bias_mlp,
        grad_b_up,
        grad_b_down,
        grad_gain_head,
        grad_bias_head,
        grad_w_head,
    )
    whole = jnp.concatenate([grad_b_head, grad_w_conv.reshape(-1), grad_b_conv])
    packed = [v.reshape(devices, -1) for v in vectors]
    packed.append(jnp.broadcast_to(whole[None], (devices, whole.shape[0])))
    packed = jnp.concatenate(packed, axis=1)
    tile = 8 * LANES
    packed = jnp.pad(packed, ((0, 0), (0, -packed.shape[1] % tile)))
    packed = packed.reshape(-1, LANES)
    sum_small = Scatter(line, packed, True, F32)
    sum_small.advance()
    sum_up.advance()
    sum_q.advance()
    sum_skip.advance()
    sum_small.advance()
    sum_kv.advance()
    skip_here = lax.optimization_barrier((skip_here, *line))[0]
    grad_joined = back_project(skip_here.reshape(rows, width), w_skip).reshape(2, block, 2 * width)
    image_shape = image_tokens.shape
    grad_image = grad_joined[:, :image_dev, :width].reshape(image_shape)
    grad_image_skip = grad_joined[:, :image_dev, width:].reshape(image_shape)
    grad_text = grad_joined[:, image_dev : image_dev + text_dev, :width]
    grad_text_skip = grad_joined[:, image_dev : image_dev + text_dev, width:]

    sum_proj.advance()
    sum_q.advance()
    sum_skip.advance()
    sum_small.advance()
    sum_kv.advance()
    sum_skip.advance()
    sum_small.advance()
    down_done, up_done, proj_done = sum_down.finish(), sum_up.finish(), sum_proj.finish()
    q_done, kv_done, skip_done = sum_q.finish(), sum_kv.finish(), sum_skip.finish()
    packed = sum_small.finish().reshape(-1)
    small = []
    start = 0
    for v in vectors:
        size = v.size // devices
        small.append(packed[start : start + size])
        start += size
    small[-1] = small[-1].reshape(-1, grad_w_head.shape[1])
    whole = packed[start : start + whole.shape[0]]
    patch_size = grad_b_head.shape[0]
    taps = grad_w_conv.size
    return (
        prediction,
        text_out,
        grad_image,
        grad_text,
        grad_image_skip,
        grad_text_skip,
        skip_done,
        small[0],
        small[1],
        small[2],
        jnp.concatenate([q_done, kv_done], axis=1),
        proj_done,
        small[3],
        small[4],
        small[5],
        up_done,
        small[6],
        down_done,
        small[7],
        small[8],
        small[9],
        small[10],
        whole[:patch_size],
        whole[patch_size : patch_size + taps].reshape(LAT_CH, LAT_CH, 3, 3),
        whole[patch_size + taps :],
    )


def solution(mesh):
    rows = P(("gx", "gy"))
    image = P("gx", None, "gy", None)
    text = P("gx", "gy", None)
    latent = P("gx", None, None, "gy")
    return jax.shard_map(
        per_device,
        mesh=mesh,
        in_specs=(image, text, image, text, P("gx"), P("gx"), latent, text) + (P(),) * 19,
        out_specs=(latent, text, image, text, image, text) + (rows,) * 16 + (P(),) * 3,
        check_vma=False,
    )
```

```python
from functools import partial
import math

import jax
import jax.numpy as jnp
from jax import lax
from jax.experimental import pallas as pl
from jax.experimental.pallas import tpu as pltpu
from jax.sharding import PartitionSpec as P

HEADS = 16
HEAD_DIM = 72
LAT_CH = 4
PATCH = 2
LANES = 128
NT = (((1,), (1,)), ((), ()))
TN = (((0,), (0,)), ((), ()))
NN = (((1,), (0,)), ((), ()))

EPSILON = 1e-05
HIGHEST = lax.Precision.HIGHEST
F32 = jnp.float32
BF16 = jnp.bfloat16
COVER = pl.CostEstimate(flops=1 << 20, transcendentals=0, bytes_accessed=1 << 20)


def bits_of(count):
    bits = count.bit_length() - 1
    assert 1 << bits == count
    return bits


def with_halo(block, axis, dim, width):
    count = lax.axis_size(axis)
    forward = [(i, i + 1) for i in range(count - 1)]
    backward = [(target, source) for source, target in forward]
    low = lax.ppermute(
        lax.slice_in_dim(block, block.shape[dim] - width, None, axis=dim), axis, forward
    )
    high = lax.ppermute(lax.slice_in_dim(block, 0, width, axis=dim), axis, backward)
    return jnp.concatenate([low, block, high], axis=dim)


def layer_norm(values, gain, bias):
    centre = jnp.mean(values, axis=-1, keepdims=True)
    centred = values - centre
    variance = jnp.mean(centred * centred, axis=-1, keepdims=True)
    return centred * lax.rsqrt(variance + EPSILON) * gain + bias


def time_embedding(time_steps, model_width):
    half_width = model_width // 2
    freqs = jnp.exp(-math.log(10000.0) * jnp.arange(half_width, dtype=F32) / half_width)
    angles = time_steps.astype(F32)[:, None] * freqs[None, :]
    return jnp.concatenate([jnp.cos(angles), jnp.sin(angles)], axis=1)


ERFC = (
    -1.26551223,
    1.00002368,
    0.37409196,
    0.09678418,
    -0.18628806,
    0.27886807,
    -1.13520398,
    1.48851587,
    -0.82215223,
    0.17087277,
)


def gelu_and_slope(values):
    u = jnp.abs(values) * math.sqrt(0.5)
    t = 1.0 / (1.0 + 0.5 * u)
    poly = jnp.full_like(t, ERFC[-1])
    for coefficient in reversed(ERFC[:-1]):
        poly = poly * t + coefficient
    bell = jnp.exp(-u * u)
    tail = 0.5 * t * bell * jnp.exp(poly)
    below = jnp.where(values < 0.0, tail, 1.0 - tail)
    return values * below, below + values * bell * (1.0 / math.sqrt(2.0 * math.pi))


def project(rows, weight):
    return jnp.einsum("rd,de->re", rows, weight, preferred_element_type=F32)


def back_project(grads, weight):
    return jnp.einsum("re,de->rd", grads, weight, preferred_element_type=F32)


class Regroup:
    def __init__(self):
        self.gx, self.gy = lax.axis_size("gx"), lax.axis_size("gy")
        self.ratio = self.gy // 4
        assert self.ratio * 4 == self.gy and self.gx % 2 == 0
        core, z = lax.axis_index("gx") % 2, lax.axis_index("gy")
        self.parity = z % 2
        self.item = z // self.ratio
        self.slot = (z % self.ratio) * 2 + core
        self.holders = 2 * self.ratio
        self.perms = []
        for turn in range(2):
            pairs = []
            for gx in range(self.gx):
                pair, c = gx // 2, gx % 2
                for z in range(self.gy):
                    f = (z & 1) ^ turn
                    item, d = 2 * c + f, z // 2
                    to_z, to_c = item * self.ratio + d // 2, d % 2
                    pairs.append((gx * self.gy + z, (2 * pair + to_c) * self.gy + to_z))
            self.perms.append(pairs)

    def cut(self, blocks):
        return [
            lax.dynamic_index_in_dim(blocks, self.parity ^ turn, 0, keepdims=False)
            for turn in range(2)
        ]

    def send(self, sends):
        return [lax.ppermute(sends[t], ("gx", "gy"), self.perms[t]) for t in range(2)]

    def there(self, blocks):
        return self.send(self.cut(blocks))

    def back(self, first, second):
        got = [
            lax.ppermute(part, ("gx", "gy"), [(b, a) for a, b in self.perms[turn]])
            for turn, part in enumerate((first, second))
        ]
        even = self.parity == 0
        return jnp.stack([jnp.where(even, got[0], got[1]), jnp.where(even, got[1], got[0])])

    def share(self, rows, step):
        pairs = []
        for gx in range(self.gx):
            pair, c = gx // 2, gx % 2
            for z in range(self.gy):
                base, d = z // self.ratio * self.ratio, (z % self.ratio) * 2 + c
                to = (d + step) % self.holders
                pairs.append(
                    (gx * self.gy + z, (2 * pair + to % 2) * self.gy + base + to // 2)
                )
        return lax.ppermute(rows, ("gx", "gy"), pairs)

    def block_z(self, step, turn):
        d = (self.slot - step) % self.holders
        return 2 * d + ((self.item % 2) ^ turn)


def back_kernel(grads, weight, *refs):
    value = dot(grads[...], weight[...], NT)
    if len(refs) == 2:
        value = value * refs[0][...].astype(F32)
    refs[-1][...] = value.astype(refs[-1].dtype)


def back(grads, weight, dtype, *slope):
    count, width = grads.shape
    height = weight.shape[0]
    tile = 1152 if width == 1152 and height % 1152 == 0 else 384
    tile = tile if height % tile == 0 else height
    part = pl.BlockSpec((count, tile), lambda j: (0, j))
    return pl.pallas_call(
        back_kernel,
        out_shape=jax.ShapeDtypeStruct((count, height), dtype),
        grid=(height // tile,),
        in_specs=[
            pl.BlockSpec((count, width), lambda j: (0, 0)),
            pl.BlockSpec((tile, width), lambda j: (j, 0)),
            *[part for _ in slope],
        ],
        out_specs=part,
        compiler_params=pltpu.CompilerParams(vmem_limit_bytes=48 << 20),
        cost_estimate=COVER,
        name="back",
    )(grads, weight, *slope)


def weight_grad_kernel(pairs, block, other, rows, grads, full, send, sums):
    full[...] = dot(rows[...], grads[...], TN).astype(full.dtype)
    for pair in range(pairs):
        start = pl.multiple_of((2 * pair + other[0]) * block, 16)
        send[pair * block : (pair + 1) * block, :] = full[pl.ds(start, block), :]
    sums[...] = jnp.sum(grads[...].astype(F32), axis=0, keepdims=True)


def weight_grad(rows, grads):
    count, height = rows.shape
    width = grads.shape[1]
    block = height >> bits_of(lax.axis_size("gx"))
    tall = 1152 if height % 1152 == 0 and 1152 % (2 * block) == 0 else height
    wide = 1152 if width % 1152 == 0 else width
    other = (1 - lax.axis_index("gx") % 2).astype(jnp.int32).reshape(1)
    return pl.pallas_call(
        partial(weight_grad_kernel, tall // (2 * block), block),
        out_shape=(
            jax.ShapeDtypeStruct((height, width), BF16),
            jax.ShapeDtypeStruct((height // 2, width), BF16),
            jax.ShapeDtypeStruct((1, width), F32),
        ),
        grid_spec=pltpu.PrefetchScalarGridSpec(
            num_scalar_prefetch=1,
            grid=(height // tall, width // wide),
            in_specs=[
                pl.BlockSpec((count, tall), lambda i, j, ref: (0, i)),
                pl.BlockSpec((count, wide), lambda i, j, ref: (0, j)),
            ],
            out_specs=[
                pl.BlockSpec((tall, wide), lambda i, j, ref: (i, j)),
                pl.BlockSpec((tall // 2, wide), lambda i, j, ref: (i, j)),
                pl.BlockSpec((1, wide), lambda i, j, ref: (0, j)),
            ],
        ),
        compiler_params=pltpu.CompilerParams(vmem_limit_bytes=48 << 20),
        cost_estimate=COVER,
        name="weight_grad",
    )(other, rows, grads)


def split_kernel(count, places, rows, index, *refs):
    parts, outs, acc = refs[:count], refs[count : count + places], refs[-1]
    value = parts[0][...].astype(F32)
    for part in parts[1:]:
        value = value + part[...].astype(F32)
    acc[...] = value
    z = index[index.shape[0] - 1]
    for place in range(places):

        @pl.when(z == place)
        def _():
            for step in range(places):
                start = (place + step) % places * rows
                outs[step][...] = acc[start : start + rows, :].astype(outs[step].dtype)


def split(addends, index, places, wire):
    block, width = addends[0][0].shape[-2:]
    rows = block // places
    tile = 1152 if width % 1152 == 0 else width

    def spec(dims):
        return pl.BlockSpec(
            (None,) * len(dims) + (block, tile), lambda j, ref: (*[ref[d] for d in dims], 0, j)
        )

    return pl.pallas_call(
        partial(split_kernel, len(addends), places, rows),
        out_shape=[
            jax.ShapeDtypeStruct((rows, width), wire if step else F32) for step in range(places)
        ],
        grid_spec=pltpu.PrefetchScalarGridSpec(
            num_scalar_prefetch=1,
            grid=(width // tile,),
            in_specs=[spec(dims) for _, dims in addends],
            out_specs=[pl.BlockSpec((rows, tile), lambda j, ref: (0, j))] * places,
            scratch_shapes=[pltpu.VMEM((block, tile), F32)],
        ),
        compiler_params=pltpu.CompilerParams(vmem_limit_bytes=40 << 20),
        name="split",
    )(index, *[value for value, _ in addends])


class Scatter:
    def __init__(self, line, part, falling, wire=BF16, first=None):
        self.gx, self.gy = lax.axis_size("gx"), lax.axis_size("gy")
        bits = bits_of(self.gx)
        rest = range(1, bits)
        self.stages = [0] + list(reversed(rest) if falling else rest) + [None]
        block = part.shape[0] >> bits
        dims = list(reversed(range(bits)))
        self.addends = [(part.reshape((2,) * bits + (block, part.shape[1])), dims)]
        self.fixed, self.first = {}, first
        self.line, self.wire = line, wire

    def mine(self, bit):
        return (lax.axis_index("gx") >> bit) & 1

    def total(self, chosen):
        out = None
        for value, dims in self.addends:
            tail = value.shape[len(dims) :]
            starts = [chosen.get(d, 0) for d in dims] + [0] * len(tail)
            shape = tuple(1 if d in chosen else 2 for d in dims) + tail
            value = lax.dynamic_slice(value, [jnp.int32(i) for i in starts], shape)
            value = value.reshape(tuple(2 for d in dims if d not in chosen) + tail)
            out = value if out is None else out.astype(F32) + value.astype(F32)
        return out

    def cut(self, after):
        bit = self.bit = self.stages.pop(0)
        if bit == 0 and self.first is not None:
            return [self.first]
        newest, dims = self.addends[-1]
        newest = lax.optimization_barrier((newest, *after, *self.line))[0]
        self.addends[-1] = (newest, dims)
        if bit is not None:
            send = self.total({**self.fixed, bit: 1 - self.mine(bit)}).astype(self.wire)
            return [send.reshape(-1, send.shape[-1])]
        z = lax.axis_index("gy")
        block, width = self.addends[0][0].shape[-2:]
        rows = block // self.gy
        if rows % 8:
            bits = bits_of(self.gx)
            index = jnp.stack([self.mine(d) for d in range(bits)] + [z]).astype(jnp.int32)
            self.keep, *sends = split(self.addends, index, self.gy, self.wire)
            return sends
        shares = []
        whole = self.addends
        for step in range(self.gy):
            place = lax.rem(z + step, self.gy)
            self.addends = [
                (value.reshape(value.shape[:-2] + (self.gy, rows, width)), dims) for value, dims in whole
            ]
            out = None
            for value, dims in self.addends:
                starts = [jnp.int32(self.fixed[d]) for d in dims] + [place, 0, 0]
                value = lax.dynamic_slice(
                    value, [jnp.int32(i) for i in starts], (1,) * (len(dims) + 1) + (rows, width)
                ).reshape(rows, width)
                out = value if out is None else out.astype(F32) + value.astype(F32)
            shares.append(out.astype(self.wire) if step else out.astype(F32))
        self.keep, *sends = shares
        return sends

    def send(self, sends):
        if self.bit is None:
            self.got = [
                lax.ppermute(value, "gy", [(i, (i + step) % self.gy) for i in range(self.gy)])
                for step, value in enumerate(sends, 1)
            ]
            return
        bit = self.bit
        pairs = [(i, i ^ (1 << bit)) for i in range(self.gx)]
        got = lax.ppermute(sends[0], "gx", pairs)
        dims = [d for d in reversed(range(bits_of(self.gx))) if d not in self.fixed and d != bit]
        tail = self.addends[0][0].shape[-2:]
        self.addends.append((got.reshape((2,) * len(dims) + tail), dims))
        self.fixed[bit] = self.mine(bit)

    def advance(self, *others, after=()):
        sends = self.cut(after)
        count = len(sends)
        out = lax.optimization_barrier((*sends, *others))
        self.send(out[:count])
        self.line[:] = [out[count - 1]]
        return out[count:] if len(others) != 1 else out[-1]

    def finish(self):
        while self.stages:
            self.advance()
        out = self.keep
        for got in lax.optimization_barrier((*self.got, *self.line))[: len(self.got)]:
            out = out + got.astype(F32)
        return out


IN_VMEM = pl.BlockSpec(memory_space=pltpu.VMEM)


def dot(left, right, dims):
    return lax.dot_general(left, right, dims, preferred_element_type=F32)


def head_of(ref, head, base=0):
    start = base + head * HEAD_DIM
    return ref[:, start : start + HEAD_DIM].astype(F32)


def widen(value, extras=()):
    rows = value.shape[0]
    out = jnp.concatenate([value, jnp.zeros((rows, LANES - HEAD_DIM), F32)], axis=1)
    lane = lax.broadcasted_iota(jnp.int32, (rows, LANES), 1)
    for i, extra in enumerate(extras):
        out = jnp.where(lane == HEAD_DIM + i, extra, out)
    return out


def thirds(value):
    high = value.astype(BF16).astype(F32)
    rest = value - high
    middle = rest.astype(BF16).astype(F32)
    return high, middle, rest - middle


def attend_kernel(holders, width, chunk, *refs):
    qkv, others, bias, mixed, lse = refs[0], refs[1:holders], refs[holders], *refs[holders + 1 : holders + 3]
    q_s, k_s, v_s, o_s = refs[holders + 3 :]
    rows = qkv.shape[0]
    factor = HEAD_DIM**-0.5 * math.log2(math.e)
    for head in range(HEADS):
        q_s[head] = widen(head_of(qkv, head), (1.0,)).astype(BF16)
        for s in range(holders):
            source, base = (qkv, width) if s == 0 else (others[s - 1], 0)
            part = slice(s * rows, (s + 1) * rows)
            k_s[head, part, :] = widen(head_of(source, head, base), (bias[part, 0:1],)).astype(BF16)
            v_s[head, part, :] = widen(head_of(source, head, base + width), (1.0,)).astype(BF16)
    lane = lax.broadcasted_iota(jnp.int32, (chunk, LANES), 1)

    def one_head(head, carry):
        k, v = k_s[head], v_s[head]
        for r in range(0, rows, chunk):
            scores = dot(q_s[head, r : r + chunk, :], k, NT)
            largest = jnp.max(scores, axis=1, keepdims=True)
            expo = jnp.exp2((scores - largest) * factor).astype(BF16)
            out = dot(expo, v, NN)
            total = out[:, HEAD_DIM : HEAD_DIM + 1]
            o_s[head, r : r + chunk, :] = jnp.where(
                lane == HEAD_DIM, largest * factor + jnp.log2(total), out / total
            )
        return carry

    lax.fori_loop(0, HEADS, one_head, 0)
    lane = lax.broadcasted_iota(jnp.int32, (rows, LANES), 1)
    logs = jnp.zeros((rows, LANES), F32)
    for head in range(HEADS):
        out = o_s[head]
        mixed[:, head * HEAD_DIM : (head + 1) * HEAD_DIM] = out[:, :HEAD_DIM].astype(mixed.dtype)
        logs = jnp.where(lane == head, out[:, HEAD_DIM : HEAD_DIM + 1], logs)
    lse[...] = logs


def attend(qkv, others, bias):
    rows, width, holders = qkv.shape[0], qkv.shape[1] // 3, len(others) + 1
    keys = rows * holders
    return pl.pallas_call(
        partial(attend_kernel, holders, width, 288),
        out_shape=(
            jax.ShapeDtypeStruct((rows, width), BF16),
            jax.ShapeDtypeStruct((rows, LANES), F32),
        ),
        in_specs=[IN_VMEM] * (holders + 1),
        out_specs=(IN_VMEM,) * 2,
        scratch_shapes=[
            pltpu.VMEM((HEADS, rows, LANES), BF16),
            pltpu.VMEM((HEADS, keys, LANES), BF16),
            pltpu.VMEM((HEADS, keys, LANES), BF16),
            pltpu.VMEM((HEADS, rows, LANES), F32),
        ],
        cost_estimate=COVER,
        compiler_params=pltpu.CompilerParams(vmem_limit_bytes=56 << 20),
        name="attend",
    )(qkv, *others, bias)


def attend_back_kernel(holders, width, chunk, first, heads, *refs):
    refs = list(refs)
    qkv, others, bias, mixed, lse, grad = refs[0], refs[1:holders], *refs[holders : holders + 4]
    refs = refs[holders + 4 :]
    last = first + heads == HEADS
    earlier, refs = (refs[:2], refs[2:]) if last and first else ((), refs)
    outs, refs = (refs[: holders + 1], refs[holders + 1 :]) if last else (refs[:2], refs[2:])
    q_s, k_s, v_s, g_s = refs[:4]
    dq_s, dkv_s = refs[4:] if last else outs
    rows = qkv.shape[0]
    keys = rows * holders
    scale = HEAD_DIM**-0.5
    factor = scale * math.log2(math.e)
    for i in range(heads):
        head = first + i
        g = head_of(grad, head)
        delta = jnp.sum(g * head_of(mixed, head), axis=1, keepdims=True)
        shift = thirds(lse[:, head : head + 1] * (-1.0 / factor))
        q_s[i] = widen(head_of(qkv, head), (1.0,) + shift).astype(BF16)
        g_s[i] = widen(g, thirds(-delta)).astype(BF16)
        for s in range(holders):
            source, base = (qkv, width) if s == 0 else (others[s - 1], 0)
            part = slice(s * rows, (s + 1) * rows)
            k = widen(head_of(source, head, base), (bias[part, 0:1], 1.0, 1.0, 1.0))
            k_s[i, part, :] = k.astype(BF16)
            v_s[i, part, :] = widen(head_of(source, head, base + width), (1.0,) * 3).astype(BF16)

    def one_head(i, carry):
        q, g = q_s[i], g_s[i]
        dq = jnp.zeros((LANES, rows), F32)
        for r in range(0, keys, chunk):
            k, v = k_s[i, r : r + chunk, :], v_s[i, r : r + chunk, :]
            probs = jnp.exp2(dot(k, q, NT) * factor)
            ds = (probs * dot(v, g, NT)).astype(BF16)
            dkv_s[0, i, r : r + chunk, :] = (dot(ds, q, NN) * scale).astype(dkv_s.dtype)
            dkv_s[1, i, r : r + chunk, :] = dot(probs.astype(BF16), g, NN).astype(dkv_s.dtype)
            dq = dq + dot(k, ds, TN)
        dq_s[i] = (jnp.transpose(dq) * scale).astype(dq_s.dtype)
        return carry

    lax.fori_loop(0, heads, one_head, 0)
    if not last:
        return
    for head in range(HEADS):
        dq, dkv, i = (dq_s, dkv_s, head - first) if head >= first else (*earlier, head)
        cols = slice(head * HEAD_DIM, (head + 1) * HEAD_DIM)
        outs[0][:, cols] = dq[i][:, :HEAD_DIM].astype(F32).astype(BF16)
        for s in range(holders):
            for which in range(2):
                value = dkv[which, i, s * rows : (s + 1) * rows, :][:, :HEAD_DIM]
                cols = slice(which * width + head * HEAD_DIM, which * width + (head + 1) * HEAD_DIM)
                outs[1 + s][:, cols] = value.astype(F32).astype(BF16)


def attend_back(qkv, others, bias, mixed, lse, grad, first, heads, earlier):
    rows, width, holders = qkv.shape[0], qkv.shape[1] // 3, len(others) + 1
    keys = rows * holders
    last = first + heads == HEADS
    if last:
        out_shape = (jax.ShapeDtypeStruct((rows, width), BF16),) + (
            jax.ShapeDtypeStruct((rows, 2 * width), BF16),
        ) * holders
    else:
        out_shape = (
            jax.ShapeDtypeStruct((heads, rows, LANES), BF16),
            jax.ShapeDtypeStruct((2, heads, keys, LANES), BF16),
        )
    scratch = [
        pltpu.VMEM((heads, rows, LANES), BF16),
        pltpu.VMEM((heads, keys, LANES), BF16),
        pltpu.VMEM((heads, keys, LANES), BF16),
        pltpu.VMEM((heads, rows, LANES), BF16),
    ]
    if last:
        scratch += [
            pltpu.VMEM((heads, rows, LANES), BF16),
            pltpu.VMEM((2, heads, keys, LANES), BF16),
        ]
    return pl.pallas_call(
        partial(attend_back_kernel, holders, width, keys // 2, first, heads),
        out_shape=out_shape,
        in_specs=[IN_VMEM] * (holders + 4 + len(earlier)),
        out_specs=(IN_VMEM,) * len(out_shape),
        scratch_shapes=scratch,
        cost_estimate=COVER,
        compiler_params=pltpu.CompilerParams(vmem_limit_bytes=58 << 20),
        name="attend_back",
    )(qkv, *others, bias, mixed, lse, grad, *earlier)


def per_device(
    image_tokens,
    text_tokens,
    image_skip,
    text_skip,
    time_steps,
    caption_len,
    pred_grad,
    text_grad,
    w_skip,
    b_skip,
    gain_attn,
    bias_attn,
    w_qkv,
    w_proj,
    b_proj,
    gain_mlp,
    bias_mlp,
    w_up,
    b_up,
    w_down,
    b_down,
    gain_head,
    bias_head,
    w_head,
    b_head,
    w_conv,
    b_conv,
):
    item_count, text_dev, width = text_tokens.shape
    grid_rows, grid_cols = (image_tokens.shape[1], image_tokens.shape[2])
    image_dev = grid_rows * grid_cols
    assert item_count == 2
    block = -(-(image_dev + text_dev) // 16) * 16
    text_pad = block - image_dev
    rows = 2 * block
    go = Regroup()
    devices = go.gx * go.gy

    caption = jnp.broadcast_to(caption_len.astype(F32)[:, None, None], (2, 1, width))
    message = go.there(jnp.concatenate([text_grad, caption], axis=1))

    slots = lax.axis_index("gy") * text_dev + jnp.arange(text_dev, dtype=jnp.int32)
    first_row = (slots == 0).astype(F32)
    embed = time_embedding(time_steps, width)
    text_in = (text_tokens.astype(F32) + first_row[None, :, None] * embed[:, None, :]).astype(BF16)

    def rows_of(image, text):
        return jnp.concatenate(
            [
                image.reshape(item_count, image_dev, width),
                jnp.pad(text, ((0, 0), (0, text_pad - text_dev), (0, 0))),
            ],
            axis=1,
        )

    joined_here = jnp.concatenate(
        [rows_of(image_tokens, text_in), rows_of(image_skip, text_skip)], axis=2
    )
    resid_here = (
        project(joined_here.reshape(rows, 2 * width), w_skip) + b_skip
    ).astype(BF16)
    away = go.cut(resid_here.reshape(2, block, width))
    *away, pred_grad = lax.optimization_barrier((*away, pred_grad))
    lat_shape = pred_grad.shape
    lat_rows, lat_cols = (lat_shape[2], lat_shape[3])
    grad_pad = jnp.pad(with_halo(pred_grad, "gy", 3, 1), ((0, 0), (0, 0), (1, 1), (0, 0)))
    grad_latent = jnp.zeros(lat_shape, F32)
    for row_off in range(3):
        for col_off in range(3):
            grad_latent = grad_latent + jnp.einsum(
                "oi,bohw->bihw",
                w_conv[:, :, row_off, col_off],
                grad_pad[
                    :, :, 2 - row_off : 2 - row_off + lat_rows, 2 - col_off : 2 - col_off + lat_cols
                ],
                precision=HIGHEST,
            )
    grad_patches = jnp.transpose(
        grad_latent.reshape(item_count, LAT_CH, grid_rows, PATCH, grid_cols, PATCH),
        (0, 2, 4, 3, 5, 1),
    ).reshape(item_count, image_dev, LAT_CH * PATCH * PATCH)
    grad_b_head = jnp.sum(grad_patches, axis=(0, 1))
    grad_b_conv = jnp.sum(pred_grad, axis=(0, 2, 3))

    resid = jnp.concatenate(go.send(away), axis=0).astype(F32)
    resid, joined_late, grad_patches = lax.optimization_barrier((resid, joined_here, grad_patches))
    joined = go.there(joined_late)
    patch_rows = -(-grad_patches.shape[1] * grad_patches.shape[2] // LANES)
    flat = grad_patches.reshape(2, -1)
    flat = jnp.pad(flat, ((0, 0), (0, patch_rows * LANES - flat.shape[1])))
    grad_patches = jnp.concatenate(
        [
            part.reshape(-1)[: image_dev * 16].reshape(-1, 16)
            for part in go.there(flat.reshape(2, patch_rows, LANES))
        ],
        axis=0,
    )
    text_grad_rows = [part[:text_dev] for part in message]
    caption = message[0][-1, 0].astype(jnp.int32)

    normed_attn, attn_norm_back = jax.vjp(layer_norm, resid, gain_attn, bias_attn)
    normed = normed_attn.astype(BF16)
    qkv = project(normed, w_qkv).astype(BF16)
    key_values = qkv[:, width:]
    others = [go.share(key_values, step) for step in range(1, go.holders)]
    inside = jnp.arange(text_pad, dtype=jnp.int32)
    bias = []
    for step in range(go.holders):
        for turn in range(2):
            slot = go.block_z(step, turn) * text_dev + inside
            allowed = (inside < text_dev) & (slot <= caption)
            bias += [jnp.zeros((image_dev,), F32), jnp.where(allowed, 0.0, -1e30)]
    bias = jnp.broadcast_to(jnp.concatenate(bias)[:, None], (rows * go.holders, LANES))
    mixed, lse = attend(qkv, others, bias)

    resid_two = resid + project(mixed, w_proj) + b_proj
    normed_mlp, mlp_norm_back = jax.vjp(layer_norm, resid_two, gain_mlp, bias_mlp)
    normed_two = normed_mlp.astype(BF16)
    pre_act = project(normed_two, w_up) + b_up
    activated, slope = gelu_and_slope(pre_act)
    hidden, slope = activated.astype(BF16), slope.astype(BF16)
    hidden, slope, *joined = lax.optimization_barrier((hidden, slope, *joined))
    joined = jnp.concatenate(joined, axis=0)
    resid_three = resid_two + project(hidden, w_down) + b_down

    def image_of(values):
        return jnp.concatenate([values[:image_dev], values[block : block + image_dev]], axis=0)

    def text_of(values):
        return [values[image_dev : image_dev + text_dev], values[block + image_dev : block + image_dev + text_dev]]

    text_out = go.back(*[part.astype(BF16) for part in text_of(resid_three)])
    normed_head, head_norm_back = jax.vjp(layer_norm, image_of(resid_three), gain_head, bias_head)
    head_in = normed_head.astype(BF16)
    patches = project(head_in, w_head) + b_head
    patches = go.back(patches[:image_dev], patches[image_dev:])

    grad_w_head = jnp.einsum("rd,ro->do", head_in.astype(F32), grad_patches, precision=HIGHEST)
    grad_normed_head = jnp.einsum("ro,do->rd", grad_patches, w_head.astype(F32), precision=HIGHEST)
    grad_image_out, grad_gain_head, grad_bias_head = head_norm_back(grad_normed_head)
    text_padding = ((0, text_pad - text_dev), (0, 0))
    grad_three = jnp.concatenate(
        [
            grad_image_out[:image_dev],
            jnp.pad(text_grad_rows[0], text_padding),
            grad_image_out[image_dev:],
            jnp.pad(text_grad_rows[1], text_padding),
        ],
        axis=0,
    )
    grad_b_down = jnp.sum(grad_three, axis=0)
    line = []

    def scatter(left, right, falling):
        full, first, sums = weight_grad(left, right)
        return Scatter(line, full, falling, BF16, first), sums[0]

    down_in = grad_three.astype(BF16)
    sum_down, _ = scatter(hidden, down_in, False)
    down_in = sum_down.advance(down_in)
    pre_low = back(down_in, w_down, BF16, slope)
    pre_low = sum_down.advance(pre_low)
    sum_up, grad_b_up = scatter(normed_two, pre_low, True)
    pre_low = sum_up.advance(pre_low)
    grad_two, grad_gain_mlp, grad_bias_mlp = mlp_norm_back(back(pre_low, w_up, F32))
    grad_two = grad_two + grad_three
    grad_b_proj = jnp.sum(grad_two, axis=0)
    proj_in = grad_two.astype(BF16)
    proj_in = sum_up.advance(proj_in)
    sum_proj, _ = scatter(mixed, proj_in, False)
    proj_in = sum_proj.advance(proj_in)
    grad_mixed = back(proj_in, w_proj, BF16)
    grad_mixed, text_out, patches = lax.optimization_barrier((grad_mixed, text_out, patches))
    patch_grid = patches.reshape(item_count, grid_rows, grid_cols, PATCH, PATCH, LAT_CH)
    latent = jnp.transpose(patch_grid, (0, 5, 1, 3, 2, 4)).reshape(lat_shape)
    padded = jnp.pad(with_halo(latent, "gy", 3, 1), ((0, 0), (0, 0), (1, 1), (0, 0)))
    prediction = jnp.zeros(lat_shape, F32) + b_conv[None, :, None, None]
    conv_taps = []
    for row_off in range(3):
        for col_off in range(3):
            window = padded[:, :, row_off : row_off + lat_rows, col_off : col_off + lat_cols]
            prediction = prediction + jnp.einsum(
                "oi,bihw->bohw", w_conv[:, :, row_off, col_off], window, precision=HIGHEST
            )
            conv_taps.append(jnp.einsum("bohw,bihw->oi", pred_grad, window, precision=HIGHEST))
    grad_w_conv = jnp.stack(conv_taps, axis=-1)

    parts = attend_back(qkv, others, bias, mixed, lse, grad_mixed, 0, HEADS // 2, ())
    parts = sum_proj.advance(*parts, after=parts[:1])
    parts = sum_down.advance(*parts)
    grads = attend_back(qkv, others, bias, mixed, lse, grad_mixed, HEADS // 2, HEADS // 2, parts)
    shared = [go.share(grads[1 + step], go.holders - step) for step in range(1, go.holders)]
    sum_q, _ = scatter(normed, grads[0], True)
    first = sum_q.advance(grads[1])
    first = sum_up.advance(first, after=grads[:1])
    grad_kv = first.astype(F32)
    for value in shared:
        grad_kv = grad_kv + value.astype(F32)
    grad_kv = grad_kv.astype(BF16)
    sum_kv, _ = scatter(normed, grad_kv, False)
    grad_kv = sum_kv.advance(grad_kv)
    grad_kv = sum_down.advance(grad_kv)
    grad_kv = sum_q.advance(grad_kv)
    grad_kv = sum_proj.advance(grad_kv)
    grad_qkv = jnp.concatenate([grads[0], grad_kv], axis=1)
    grad_one = back(grad_qkv, w_qkv, F32)
    grad_one = sum_kv.advance(grad_one, after=(grad_one,))
    grad_one, grad_gain_attn, grad_bias_attn = attn_norm_back(grad_one)
    grad_one = grad_one + grad_two
    grad_b_skip = jnp.sum(grad_one, axis=0)
    skip_in = grad_one.astype(BF16)
    skip_here = go.back(skip_in[:block], skip_in[block:])
    sum_skip, _ = scatter(joined, skip_in, True)
    sum_skip.advance()
    down_done = sum_down.finish()
    line.append(down_done)
    vectors = (
        grad_b_skip,
        grad_gain_attn,
        grad_bias_attn,
        grad_b_proj,
        grad_gain_mlp,
        grad_bias_mlp,
        grad_b_up,
        grad_b_down,
        grad_gain_head,
        grad_bias_head,
        grad_w_head,
    )
    whole = jnp.concatenate([grad_b_head, grad_w_conv.reshape(-1), grad_b_conv])
    packed = [v.reshape(devices, -1) for v in vectors]
    packed.append(jnp.broadcast_to(whole[None], (devices, whole.shape[0])))
    packed = jnp.concatenate(packed, axis=1)
    tile = 8 * LANES
    packed = jnp.pad(packed, ((0, 0), (0, -packed.shape[1] % tile)))
    packed = packed.reshape(-1, LANES)
    sum_small = Scatter(line, packed, True, F32)
    sum_small.advance()
    sum_up.advance()
    sum_q.advance()
    sum_skip.advance()
    sum_small.advance()
    sum_kv.advance()
    skip_here = lax.optimization_barrier((skip_here, *line))[0]
    grad_joined = back_project(skip_here.reshape(rows, width), w_skip).reshape(2, block, 2 * width)
    image_shape = image_tokens.shape
    grad_image = grad_joined[:, :image_dev, :width].reshape(image_shape)
    grad_image_skip = grad_joined[:, :image_dev, width:].reshape(image_shape)
    grad_text = grad_joined[:, image_dev : image_dev + text_dev, :width]
    grad_text_skip = grad_joined[:, image_dev : image_dev + text_dev, width:]

    sum_proj.advance()
    sum_q.advance()
    sum_skip.advance()
    sum_small.advance()
    sum_kv.advance()
    sum_skip.advance()
    sum_small.advance()
    up_done, proj_done = sum_up.finish(), sum_proj.finish()
    q_done, kv_done, skip_done = sum_q.finish(), sum_kv.finish(), sum_skip.finish()
    packed = sum_small.finish().reshape(-1)
    small = []
    start = 0
    for v in vectors:
        size = v.size // devices
        small.append(packed[start : start + size])
        start += size
    small[-1] = small[-1].reshape(-1, grad_w_head.shape[1])
    whole = packed[start : start + whole.shape[0]]
    patch_size = grad_b_head.shape[0]
    taps = grad_w_conv.size
    return (
        prediction,
        text_out,
        grad_image,
        grad_text,
        grad_image_skip,
        grad_text_skip,
        skip_done,
        small[0],
        small[1],
        small[2],
        jnp.concatenate([q_done, kv_done], axis=1),
        proj_done,
        small[3],
        small[4],
        small[5],
        up_done,
        small[6],
        down_done,
        small[7],
        small[8],
        small[9],
        small[10],
        whole[:patch_size],
        whole[patch_size : patch_size + taps].reshape(LAT_CH, LAT_CH, 3, 3),
        whole[patch_size + taps :],
    )


def solution(mesh):
    rows = P(("gx", "gy"))
    image = P("gx", None, "gy", None)
    text = P("gx", "gy", None)
    latent = P("gx", None, None, "gy")
    return jax.shard_map(
        per_device,
        mesh=mesh,
        in_specs=(image, text, image, text, P("gx"), P("gx"), latent, text) + (P(),) * 19,
        out_specs=(latent, text, image, text, image, text) + (rows,) * 16 + (P(),) * 3,
        check_vma=False,
    )
```

```python
from functools import partial
import math

import jax
import jax.numpy as jnp
from jax import lax
from jax.experimental import pallas as pl
from jax.experimental.pallas import tpu as pltpu
from jax.sharding import PartitionSpec as P

HEADS = 16
HEAD_DIM = 72
LAT_CH = 4
PATCH = 2
LANES = 128
NT = (((1,), (1,)), ((), ()))
TN = (((0,), (0,)), ((), ()))
NN = (((1,), (0,)), ((), ()))

EPSILON = 1e-05
HIGHEST = lax.Precision.HIGHEST
F32 = jnp.float32
BF16 = jnp.bfloat16
COVER = pl.CostEstimate(flops=1 << 20, transcendentals=0, bytes_accessed=1 << 20)


def bits_of(count):
    bits = count.bit_length() - 1
    assert 1 << bits == count
    return bits


def with_halo(block, axis, dim, width):
    count = lax.axis_size(axis)
    forward = [(i, i + 1) for i in range(count - 1)]
    backward = [(target, source) for source, target in forward]
    low = lax.ppermute(
        lax.slice_in_dim(block, block.shape[dim] - width, None, axis=dim), axis, forward
    )
    high = lax.ppermute(lax.slice_in_dim(block, 0, width, axis=dim), axis, backward)
    return jnp.concatenate([low, block, high], axis=dim)


def layer_norm(values, gain, bias):
    centre = jnp.mean(values, axis=-1, keepdims=True)
    centred = values - centre
    variance = jnp.mean(centred * centred, axis=-1, keepdims=True)
    return centred * lax.rsqrt(variance + EPSILON) * gain + bias


def time_embedding(time_steps, model_width):
    half_width = model_width // 2
    freqs = jnp.exp(-math.log(10000.0) * jnp.arange(half_width, dtype=F32) / half_width)
    angles = time_steps.astype(F32)[:, None] * freqs[None, :]
    return jnp.concatenate([jnp.cos(angles), jnp.sin(angles)], axis=1)


ERFC = (
    -1.26551223,
    1.00002368,
    0.37409196,
    0.09678418,
    -0.18628806,
    0.27886807,
    -1.13520398,
    1.48851587,
    -0.82215223,
    0.17087277,
)


def gelu_and_slope(values):
    t = 1.0 / (1.0 + (0.5 * math.sqrt(0.5)) * jnp.abs(values))
    poly = jnp.full_like(t, ERFC[-1])
    for coefficient in reversed((ERFC[0] + math.log(0.5),) + ERFC[1:-1]):
        poly = poly * t + coefficient
    bell = jnp.exp(-0.5 * (values * values))
    tail = t * bell * jnp.exp(poly)
    below = jnp.where(values < 0.0, tail, 1.0 - tail)
    return values * below, below + values * bell * (1.0 / math.sqrt(2.0 * math.pi))


def project(rows, weight):
    return jnp.einsum("rd,de->re", rows, weight, preferred_element_type=F32)


def back_project(grads, weight):
    return jnp.einsum("re,de->rd", grads, weight, preferred_element_type=F32)


class Regroup:
    def __init__(self):
        self.gx, self.gy = lax.axis_size("gx"), lax.axis_size("gy")
        self.ratio = self.gy // 4
        assert self.ratio * 4 == self.gy and self.gx % 2 == 0
        core, z = lax.axis_index("gx") % 2, lax.axis_index("gy")
        self.parity = z % 2
        self.item = z // self.ratio
        self.slot = (z % self.ratio) * 2 + core
        self.holders = 2 * self.ratio
        self.perms = []
        for turn in range(2):
            pairs = []
            for gx in range(self.gx):
                pair, c = gx // 2, gx % 2
                for z in range(self.gy):
                    f = (z & 1) ^ turn
                    item, d = 2 * c + f, z // 2
                    to_z, to_c = item * self.ratio + d // 2, d % 2
                    pairs.append((gx * self.gy + z, (2 * pair + to_c) * self.gy + to_z))
            self.perms.append(pairs)

    def cut(self, blocks):
        return [
            lax.dynamic_index_in_dim(blocks, self.parity ^ turn, 0, keepdims=False)
            for turn in range(2)
        ]

    def send(self, sends):
        return [lax.ppermute(sends[t], ("gx", "gy"), self.perms[t]) for t in range(2)]

    def there(self, blocks):
        return self.send(self.cut(blocks))

    def back(self, first, second):
        got = [
            lax.ppermute(part, ("gx", "gy"), [(b, a) for a, b in self.perms[turn]])
            for turn, part in enumerate((first, second))
        ]
        even = self.parity == 0
        return jnp.stack([jnp.where(even, got[0], got[1]), jnp.where(even, got[1], got[0])])

    def share(self, rows, step):
        pairs = []
        for gx in range(self.gx):
            pair, c = gx // 2, gx % 2
            for z in range(self.gy):
                base, d = z // self.ratio * self.ratio, (z % self.ratio) * 2 + c
                to = (d + step) % self.holders
                pairs.append(
                    (gx * self.gy + z, (2 * pair + to % 2) * self.gy + base + to // 2)
                )
        return lax.ppermute(rows, ("gx", "gy"), pairs)

    def block_z(self, step, turn):
        d = (self.slot - step) % self.holders
        return 2 * d + ((self.item % 2) ^ turn)


def back_kernel(grads, weight, *refs):
    value = dot(grads[...], weight[...], NT)
    if len(refs) == 2:
        value = value * refs[0][...].astype(F32)
    refs[-1][...] = value.astype(refs[-1].dtype)


def back(grads, weight, dtype, *slope):
    count, width = grads.shape
    height = weight.shape[0]
    tile = 1152 if width == 1152 and height % 1152 == 0 else 384
    tile = tile if height % tile == 0 else height
    part = pl.BlockSpec((count, tile), lambda j: (0, j))
    return pl.pallas_call(
        back_kernel,
        out_shape=jax.ShapeDtypeStruct((count, height), dtype),
        grid=(height // tile,),
        in_specs=[
            pl.BlockSpec((count, width), lambda j: (0, 0)),
            pl.BlockSpec((tile, width), lambda j: (j, 0)),
            *[part for _ in slope],
        ],
        out_specs=part,
        compiler_params=pltpu.CompilerParams(vmem_limit_bytes=48 << 20),
        cost_estimate=COVER,
        name="back",
    )(grads, weight, *slope)


def weight_grad_kernel(pairs, block, other, rows, grads, full, send, sums):
    full[...] = dot(rows[...], grads[...], TN).astype(full.dtype)
    for pair in range(pairs):
        rows_out = slice(pair * block, (pair + 1) * block)
        if block % 16 == 0:
            start = pl.multiple_of((2 * pair + other[0]) * block, 16)
            send[rows_out, :] = full[pl.ds(start, block), :]
            continue
        low, high = (full[(2 * pair + k) * block : (2 * pair + k + 1) * block, :] for k in range(2))
        send[rows_out, :] = jnp.where(other[0] == 0, low.astype(F32), high.astype(F32)).astype(send.dtype)
    sums[...] = jnp.sum(grads[...].astype(F32), axis=0, keepdims=True)


def weight_grad(rows, grads):
    count, height = rows.shape
    width = grads.shape[1]
    block = height >> bits_of(lax.axis_size("gx"))
    tall = 1152 if height % 1152 == 0 and 1152 % (2 * block) == 0 else height
    wide = 1152 if width % 1152 == 0 else width
    other = (1 - lax.axis_index("gx") % 2).astype(jnp.int32).reshape(1)
    return pl.pallas_call(
        partial(weight_grad_kernel, tall // (2 * block), block),
        out_shape=(
            jax.ShapeDtypeStruct((height, width), BF16),
            jax.ShapeDtypeStruct((height // 2, width), BF16),
            jax.ShapeDtypeStruct((1, width), F32),
        ),
        grid_spec=pltpu.PrefetchScalarGridSpec(
            num_scalar_prefetch=1,
            grid=(height // tall, width // wide),
            in_specs=[
                pl.BlockSpec((count, tall), lambda i, j, ref: (0, i)),
                pl.BlockSpec((count, wide), lambda i, j, ref: (0, j)),
            ],
            out_specs=[
                pl.BlockSpec((tall, wide), lambda i, j, ref: (i, j)),
                pl.BlockSpec((tall // 2, wide), lambda i, j, ref: (i, j)),
                pl.BlockSpec((1, wide), lambda i, j, ref: (0, j)),
            ],
        ),
        compiler_params=pltpu.CompilerParams(vmem_limit_bytes=48 << 20),
        cost_estimate=COVER,
        name="weight_grad",
    )(other, rows, grads)


def split_kernel(count, places, rows, index, *refs):
    parts, outs, acc = refs[:count], refs[count : count + places], refs[-1]
    value = parts[0][...].astype(F32)
    for part in parts[1:]:
        value = value + part[...].astype(F32)
    acc[...] = value
    z = index[index.shape[0] - 1]
    for place in range(places):

        @pl.when(z == place)
        def _():
            for step in range(places):
                start = (place + step) % places * rows
                outs[step][...] = acc[start : start + rows, :].astype(outs[step].dtype)


def split(addends, index, places, wire):
    block, width = addends[0][0].shape[-2:]
    rows = block // places
    tile = 1152 if width % 1152 == 0 else width

    def spec(dims):
        return pl.BlockSpec(
            (None,) * len(dims) + (block, tile), lambda j, ref: (*[ref[d] for d in dims], 0, j)
        )

    return pl.pallas_call(
        partial(split_kernel, len(addends), places, rows),
        out_shape=[
            jax.ShapeDtypeStruct((rows, width), wire if step else F32) for step in range(places)
        ],
        grid_spec=pltpu.PrefetchScalarGridSpec(
            num_scalar_prefetch=1,
            grid=(width // tile,),
            in_specs=[spec(dims) for _, dims in addends],
            out_specs=[pl.BlockSpec((rows, tile), lambda j, ref: (0, j))] * places,
            scratch_shapes=[pltpu.VMEM((block, tile), F32)],
        ),
        compiler_params=pltpu.CompilerParams(vmem_limit_bytes=40 << 20),
        name="split",
    )(index, *[value for value, _ in addends])


class Scatter:
    def __init__(self, line, part, falling, wire=BF16, first=None):
        self.gx, self.gy = lax.axis_size("gx"), lax.axis_size("gy")
        bits = bits_of(self.gx)
        rest = range(1, bits)
        self.stages = [0] + list(reversed(rest) if falling else rest) + [None]
        block = part.shape[0] >> bits
        dims = list(reversed(range(bits)))
        self.addends = [(part.reshape((2,) * bits + (block, part.shape[1])), dims)]
        self.fixed, self.first = {}, first
        self.line, self.wire = line, wire

    def mine(self, bit):
        return (lax.axis_index("gx") >> bit) & 1

    def total(self, chosen):
        out = None
        for value, dims in self.addends:
            tail = value.shape[len(dims) :]
            starts = [chosen.get(d, 0) for d in dims] + [0] * len(tail)
            shape = tuple(1 if d in chosen else 2 for d in dims) + tail
            value = lax.dynamic_slice(value, [jnp.int32(i) for i in starts], shape)
            value = value.reshape(tuple(2 for d in dims if d not in chosen) + tail)
            out = value if out is None else out.astype(F32) + value.astype(F32)
        return out

    def cut(self, after):
        bit = self.bit = self.stages.pop(0)
        if bit == 0 and self.first is not None:
            return [self.first]
        newest, dims = self.addends[-1]
        newest = lax.optimization_barrier((newest, *after, *self.line))[0]
        self.addends[-1] = (newest, dims)
        if bit is not None:
            send = self.total({**self.fixed, bit: 1 - self.mine(bit)}).astype(self.wire)
            return [send.reshape(-1, send.shape[-1])]
        z = lax.axis_index("gy")
        block, width = self.addends[0][0].shape[-2:]
        rows = block // self.gy
        if rows % 8:
            bits = bits_of(self.gx)
            index = jnp.stack([self.mine(d) for d in range(bits)] + [z]).astype(jnp.int32)
            self.keep, *sends = split(self.addends, index, self.gy, self.wire)
            return sends
        shares = []
        whole = self.addends
        for step in range(self.gy):
            place = lax.rem(z + step, self.gy)
            self.addends = [
                (value.reshape(value.shape[:-2] + (self.gy, rows, width)), dims) for value, dims in whole
            ]
            out = None
            for value, dims in self.addends:
                starts = [jnp.int32(self.fixed[d]) for d in dims] + [place, 0, 0]
                value = lax.dynamic_slice(
                    value, [jnp.int32(i) for i in starts], (1,) * (len(dims) + 1) + (rows, width)
                ).reshape(rows, width)
                out = value if out is None else out.astype(F32) + value.astype(F32)
            shares.append(out.astype(self.wire) if step else out.astype(F32))
        self.keep, *sends = shares
        return sends

    def send(self, sends):
        if self.bit is None:
            self.got = [
                lax.ppermute(value, "gy", [(i, (i + step) % self.gy) for i in range(self.gy)])
                for step, value in enumerate(sends, 1)
            ]
            return
        bit = self.bit
        pairs = [(i, i ^ (1 << bit)) for i in range(self.gx)]
        got = lax.ppermute(sends[0], "gx", pairs)
        dims = [d for d in reversed(range(bits_of(self.gx))) if d not in self.fixed and d != bit]
        tail = self.addends[0][0].shape[-2:]
        self.addends.append((got.reshape((2,) * len(dims) + tail), dims))
        self.fixed[bit] = self.mine(bit)

    def advance(self, *others, after=()):
        sends = self.cut(after)
        count = len(sends)
        out = lax.optimization_barrier((*sends, *others))
        self.send(out[:count])
        self.line[:] = [out[count - 1]]
        return out[count:] if len(others) != 1 else out[-1]

    def finish(self):
        while self.stages:
            self.advance()
        out = self.keep
        for got in lax.optimization_barrier((*self.got, *self.line))[: len(self.got)]:
            out = out + got.astype(F32)
        return out


IN_VMEM = pl.BlockSpec(memory_space=pltpu.VMEM)


def dot(left, right, dims):
    return lax.dot_general(left, right, dims, preferred_element_type=F32)


def head_of(ref, head, base=0):
    start = base + head * HEAD_DIM
    return ref[:, start : start + HEAD_DIM].astype(F32)


def widen(value, extras=()):
    rows = value.shape[0]
    out = jnp.concatenate([value, jnp.zeros((rows, LANES - HEAD_DIM), F32)], axis=1)
    lane = lax.broadcasted_iota(jnp.int32, (rows, LANES), 1)
    for i, extra in enumerate(extras):
        out = jnp.where(lane == HEAD_DIM + i, extra, out)
    return out


def thirds(value):
    high = value.astype(BF16).astype(F32)
    rest = value - high
    middle = rest.astype(BF16).astype(F32)
    return high, middle, rest - middle


def attend_kernel(holders, width, chunk, *refs):
    qkv, others, bias, mixed, lse = refs[0], refs[1:holders], refs[holders], *refs[holders + 1 : holders + 3]
    q_s, k_s, v_s, o_s = refs[holders + 3 :]
    rows = qkv.shape[0]
    factor = HEAD_DIM**-0.5 * math.log2(math.e)
    for head in range(HEADS):
        q_s[head] = widen(head_of(qkv, head), (1.0,)).astype(BF16)
        for s in range(holders):
            source, base = (qkv, width) if s == 0 else (others[s - 1], 0)
            part = slice(s * rows, (s + 1) * rows)
            k_s[head, part, :] = widen(head_of(source, head, base), (bias[part, 0:1],)).astype(BF16)
            v_s[head, part, :] = widen(head_of(source, head, base + width), (1.0,)).astype(BF16)
    lane = lax.broadcasted_iota(jnp.int32, (chunk, LANES), 1)

    def one_head(head, carry):
        k, v = k_s[head], v_s[head]
        for r in range(0, rows, chunk):
            scores = dot(q_s[head, r : r + chunk, :], k, NT)
            largest = jnp.max(scores, axis=1, keepdims=True)
            expo = jnp.exp2((scores - largest) * factor).astype(BF16)
            out = dot(expo, v, NN)
            total = out[:, HEAD_DIM : HEAD_DIM + 1]
            o_s[head, r : r + chunk, :] = jnp.where(
                lane == HEAD_DIM, largest * factor + jnp.log2(total), out / total
            )
        return carry

    lax.fori_loop(0, HEADS, one_head, 0)
    lane = lax.broadcasted_iota(jnp.int32, (rows, LANES), 1)
    logs = jnp.zeros((rows, LANES), F32)
    for head in range(HEADS):
        out = o_s[head]
        mixed[:, head * HEAD_DIM : (head + 1) * HEAD_DIM] = out[:, :HEAD_DIM].astype(mixed.dtype)
        logs = jnp.where(lane == head, out[:, HEAD_DIM : HEAD_DIM + 1], logs)
    lse[...] = logs


def attend(qkv, others, bias):
    rows, width, holders = qkv.shape[0], qkv.shape[1] // 3, len(others) + 1
    keys = rows * holders
    return pl.pallas_call(
        partial(attend_kernel, holders, width, 288),
        out_shape=(
            jax.ShapeDtypeStruct((rows, width), BF16),
            jax.ShapeDtypeStruct((rows, LANES), F32),
        ),
        in_specs=[IN_VMEM] * (holders + 1),
        out_specs=(IN_VMEM,) * 2,
        scratch_shapes=[
            pltpu.VMEM((HEADS, rows, LANES), BF16),
            pltpu.VMEM((HEADS, keys, LANES), BF16),
            pltpu.VMEM((HEADS, keys, LANES), BF16),
            pltpu.VMEM((HEADS, rows, LANES), F32),
        ],
        cost_estimate=COVER,
        compiler_params=pltpu.CompilerParams(vmem_limit_bytes=56 << 20),
        name="attend",
    )(qkv, *others, bias)


def attend_back_kernel(holders, width, chunk, first, heads, *refs):
    refs = list(refs)
    qkv, others, bias, mixed, lse, grad = refs[0], refs[1:holders], *refs[holders : holders + 4]
    refs = refs[holders + 4 :]
    last = first + heads == HEADS
    earlier, refs = (refs[:2], refs[2:]) if last and first else ((), refs)
    outs, refs = (refs[: holders + 1], refs[holders + 1 :]) if last else (refs[:2], refs[2:])
    q_s, k_s, v_s, g_s = refs[:4]
    dq_s, dkv_s = refs[4:] if last else outs
    rows = qkv.shape[0]
    keys = rows * holders
    scale = HEAD_DIM**-0.5
    factor = scale * math.log2(math.e)
    for i in range(heads):
        head = first + i
        g = head_of(grad, head)
        delta = jnp.sum(g * head_of(mixed, head), axis=1, keepdims=True)
        shift = thirds(lse[:, head : head + 1] * (-1.0 / factor))
        q_s[i] = widen(head_of(qkv, head), (1.0,) + shift).astype(BF16)
        g_s[i] = widen(g, thirds(-delta)).astype(BF16)
        for s in range(holders):
            source, base = (qkv, width) if s == 0 else (others[s - 1], 0)
            part = slice(s * rows, (s + 1) * rows)
            k = widen(head_of(source, head, base), (bias[part, 0:1], 1.0, 1.0, 1.0))
            k_s[i, part, :] = k.astype(BF16)
            v_s[i, part, :] = widen(head_of(source, head, base + width), (1.0,) * 3).astype(BF16)

    def one_head(i, carry):
        q, g = q_s[i], g_s[i]
        dq = jnp.zeros((LANES, rows), F32)
        for r in range(0, keys, chunk):
            k, v = k_s[i, r : r + chunk, :], v_s[i, r : r + chunk, :]
            probs = jnp.exp2(dot(k, q, NT) * factor)
            ds = (probs * dot(v, g, NT)).astype(BF16)
            dkv_s[0, i, r : r + chunk, :] = (dot(ds, q, NN) * scale).astype(dkv_s.dtype)
            dkv_s[1, i, r : r + chunk, :] = dot(probs.astype(BF16), g, NN).astype(dkv_s.dtype)
            dq = dq + dot(k, ds, TN)
        dq_s[i] = (jnp.transpose(dq) * scale).astype(dq_s.dtype)
        return carry

    lax.fori_loop(0, heads, one_head, 0)
    if not last:
        return
    for head in range(HEADS):
        dq, dkv, i = (dq_s, dkv_s, head - first) if head >= first else (*earlier, head)
        cols = slice(head * HEAD_DIM, (head + 1) * HEAD_DIM)
        outs[0][:, cols] = dq[i][:, :HEAD_DIM].astype(F32).astype(BF16)
        for s in range(holders):
            for which in range(2):
                value = dkv[which, i, s * rows : (s + 1) * rows, :][:, :HEAD_DIM]
                cols = slice(which * width + head * HEAD_DIM, which * width + (head + 1) * HEAD_DIM)
                outs[1 + s][:, cols] = value.astype(F32).astype(BF16)


def attend_back(qkv, others, bias, mixed, lse, grad, first, heads, earlier):
    rows, width, holders = qkv.shape[0], qkv.shape[1] // 3, len(others) + 1
    keys = rows * holders
    last = first + heads == HEADS
    if last:
        out_shape = (jax.ShapeDtypeStruct((rows, width), BF16),) + (
            jax.ShapeDtypeStruct((rows, 2 * width), BF16),
        ) * holders
    else:
        out_shape = (
            jax.ShapeDtypeStruct((heads, rows, LANES), BF16),
            jax.ShapeDtypeStruct((2, heads, keys, LANES), BF16),
        )
    scratch = [
        pltpu.VMEM((heads, rows, LANES), BF16),
        pltpu.VMEM((heads, keys, LANES), BF16),
        pltpu.VMEM((heads, keys, LANES), BF16),
        pltpu.VMEM((heads, rows, LANES), BF16),
    ]
    if last:
        scratch += [
            pltpu.VMEM((heads, rows, LANES), BF16),
            pltpu.VMEM((2, heads, keys, LANES), BF16),
        ]
    return pl.pallas_call(
        partial(attend_back_kernel, holders, width, keys // 2, first, heads),
        out_shape=out_shape,
        in_specs=[IN_VMEM] * (holders + 4 + len(earlier)),
        out_specs=(IN_VMEM,) * len(out_shape),
        scratch_shapes=scratch,
        cost_estimate=COVER,
        compiler_params=pltpu.CompilerParams(vmem_limit_bytes=58 << 20),
        name="attend_back",
    )(qkv, *others, bias, mixed, lse, grad, *earlier)


def per_device(
    image_tokens,
    text_tokens,
    image_skip,
    text_skip,
    time_steps,
    caption_len,
    pred_grad,
    text_grad,
    w_skip,
    b_skip,
    gain_attn,
    bias_attn,
    w_qkv,
    w_proj,
    b_proj,
    gain_mlp,
    bias_mlp,
    w_up,
    b_up,
    w_down,
    b_down,
    gain_head,
    bias_head,
    w_head,
    b_head,
    w_conv,
    b_conv,
):
    item_count, text_dev, width = text_tokens.shape
    grid_rows, grid_cols = (image_tokens.shape[1], image_tokens.shape[2])
    image_dev = grid_rows * grid_cols
    assert item_count == 2
    block = -(-(image_dev + text_dev) // 16) * 16
    text_pad = block - image_dev
    rows = 2 * block
    go = Regroup()
    devices = go.gx * go.gy

    caption = jnp.broadcast_to(caption_len.astype(F32)[:, None, None], (2, 1, width))
    message = go.there(jnp.concatenate([text_grad, caption], axis=1))

    slots = lax.axis_index("gy") * text_dev + jnp.arange(text_dev, dtype=jnp.int32)
    first_row = (slots == 0).astype(F32)
    embed = time_embedding(time_steps, width)
    text_in = (text_tokens.astype(F32) + first_row[None, :, None] * embed[:, None, :]).astype(BF16)

    def rows_of(image, text):
        return jnp.concatenate(
            [
                image.reshape(item_count, image_dev, width),
                jnp.pad(text, ((0, 0), (0, text_pad - text_dev), (0, 0))),
            ],
            axis=1,
        )

    joined_here = jnp.concatenate(
        [rows_of(image_tokens, text_in), rows_of(image_skip, text_skip)], axis=2
    )
    resid_here = (
        project(joined_here.reshape(rows, 2 * width), w_skip) + b_skip
    ).astype(BF16)
    away = go.cut(resid_here.reshape(2, block, width))
    *away, pred_grad = lax.optimization_barrier((*away, pred_grad))
    lat_shape = pred_grad.shape
    lat_rows, lat_cols = (lat_shape[2], lat_shape[3])
    grad_pad = jnp.pad(with_halo(pred_grad, "gy", 3, 1), ((0, 0), (0, 0), (1, 1), (0, 0)))
    grad_latent = jnp.zeros(lat_shape, F32)
    for row_off in range(3):
        for col_off in range(3):
            grad_latent = grad_latent + jnp.einsum(
                "oi,bohw->bihw",
                w_conv[:, :, row_off, col_off],
                grad_pad[
                    :, :, 2 - row_off : 2 - row_off + lat_rows, 2 - col_off : 2 - col_off + lat_cols
                ],
                precision=HIGHEST,
            )
    grad_patches = jnp.transpose(
        grad_latent.reshape(item_count, LAT_CH, grid_rows, PATCH, grid_cols, PATCH),
        (0, 2, 4, 3, 5, 1),
    ).reshape(item_count, image_dev, LAT_CH * PATCH * PATCH)
    grad_b_head = jnp.sum(grad_patches, axis=(0, 1))
    grad_b_conv = jnp.sum(pred_grad, axis=(0, 2, 3))

    resid = jnp.concatenate(go.send(away), axis=0).astype(F32)
    resid, joined_late, grad_patches = lax.optimization_barrier((resid, joined_here, grad_patches))
    joined = go.there(joined_late)
    patch_rows = -(-grad_patches.shape[1] * grad_patches.shape[2] // LANES)
    flat = grad_patches.reshape(2, -1)
    flat = jnp.pad(flat, ((0, 0), (0, patch_rows * LANES - flat.shape[1])))
    grad_patches = jnp.concatenate(
        [
            part.reshape(-1)[: image_dev * 16].reshape(-1, 16)
            for part in go.there(flat.reshape(2, patch_rows, LANES))
        ],
        axis=0,
    )
    text_grad_rows = [part[:text_dev] for part in message]
    caption = message[0][-1, 0].astype(jnp.int32)

    normed_attn, attn_norm_back = jax.vjp(layer_norm, resid, gain_attn, bias_attn)
    normed = normed_attn.astype(BF16)
    qkv = project(normed, w_qkv).astype(BF16)
    key_values = qkv[:, width:]
    others = [go.share(key_values, step) for step in range(1, go.holders)]
    inside = jnp.arange(text_pad, dtype=jnp.int32)
    bias = []
    for step in range(go.holders):
        for turn in range(2):
            slot = go.block_z(step, turn) * text_dev + inside
            allowed = (inside < text_dev) & (slot <= caption)
            bias += [jnp.zeros((image_dev,), F32), jnp.where(allowed, 0.0, -1e30)]
    bias = jnp.broadcast_to(jnp.concatenate(bias)[:, None], (rows * go.holders, LANES))
    mixed, lse = attend(qkv, others, bias)

    resid_two = resid + project(mixed, w_proj) + b_proj
    normed_mlp, mlp_norm_back = jax.vjp(layer_norm, resid_two, gain_mlp, bias_mlp)
    normed_two = normed_mlp.astype(BF16)
    pre_act = project(normed_two, w_up) + b_up
    activated, slope = gelu_and_slope(pre_act)
    hidden, slope = activated.astype(BF16), slope.astype(BF16)
    hidden, slope, *joined = lax.optimization_barrier((hidden, slope, *joined))
    joined = jnp.concatenate(joined, axis=0)
    resid_three = resid_two + project(hidden, w_down) + b_down

    def image_of(values):
        return jnp.concatenate([values[:image_dev], values[block : block + image_dev]], axis=0)

    def text_of(values):
        return [values[image_dev : image_dev + text_dev], values[block + image_dev : block + image_dev + text_dev]]

    text_out = go.back(*[part.astype(BF16) for part in text_of(resid_three)])
    normed_head, head_norm_back = jax.vjp(layer_norm, image_of(resid_three), gain_head, bias_head)
    head_in = normed_head.astype(BF16)
    patches = project(head_in, w_head) + b_head
    patches = go.back(patches[:image_dev], patches[image_dev:])

    grad_w_head = jnp.einsum("rd,ro->do", head_in.astype(F32), grad_patches, precision=HIGHEST)
    grad_normed_head = jnp.einsum("ro,do->rd", grad_patches, w_head.astype(F32), precision=HIGHEST)
    grad_image_out, grad_gain_head, grad_bias_head = head_norm_back(grad_normed_head)
    text_padding = ((0, text_pad - text_dev), (0, 0))
    grad_three = jnp.concatenate(
        [
            grad_image_out[:image_dev],
            jnp.pad(text_grad_rows[0], text_padding),
            grad_image_out[image_dev:],
            jnp.pad(text_grad_rows[1], text_padding),
        ],
        axis=0,
    )
    grad_b_down = jnp.sum(grad_three, axis=0)
    line = []

    def scatter(left, right, falling):
        full, first, sums = weight_grad(left, right)
        return Scatter(line, full, falling, BF16, first), sums[0]

    down_in = grad_three.astype(BF16)
    sum_down, _ = scatter(hidden, down_in, False)
    down_in = sum_down.advance(down_in)
    pre_low = back(down_in, w_down, BF16, slope)
    pre_low = sum_down.advance(pre_low)
    sum_up, grad_b_up = scatter(normed_two, pre_low, True)
    pre_low = sum_up.advance(pre_low)
    grad_two, grad_gain_mlp, grad_bias_mlp = mlp_norm_back(back(pre_low, w_up, F32))
    grad_two = grad_two + grad_three
    grad_b_proj = jnp.sum(grad_two, axis=0)
    proj_in = grad_two.astype(BF16)
    proj_in = sum_up.advance(proj_in)
    sum_proj, _ = scatter(mixed, proj_in, False)
    proj_in = sum_proj.advance(proj_in)
    grad_mixed = back(proj_in, w_proj, BF16)
    grad_mixed, text_out, patches = lax.optimization_barrier((grad_mixed, text_out, patches))
    patch_grid = patches.reshape(item_count, grid_rows, grid_cols, PATCH, PATCH, LAT_CH)
    latent = jnp.transpose(patch_grid, (0, 5, 1, 3, 2, 4)).reshape(lat_shape)
    padded = jnp.pad(with_halo(latent, "gy", 3, 1), ((0, 0), (0, 0), (1, 1), (0, 0)))
    prediction = jnp.zeros(lat_shape, F32) + b_conv[None, :, None, None]
    conv_taps = []
    for row_off in range(3):
        for col_off in range(3):
            window = padded[:, :, row_off : row_off + lat_rows, col_off : col_off + lat_cols]
            prediction = prediction + jnp.einsum(
                "oi,bihw->bohw", w_conv[:, :, row_off, col_off], window, precision=HIGHEST
            )
            conv_taps.append(jnp.einsum("bohw,bihw->oi", pred_grad, window, precision=HIGHEST))
    grad_w_conv = jnp.stack(conv_taps, axis=-1)

    parts = attend_back(qkv, others, bias, mixed, lse, grad_mixed, 0, HEADS // 2, ())
    parts = sum_proj.advance(*parts, after=parts[:1])
    parts = sum_down.advance(*parts)
    grads = attend_back(qkv, others, bias, mixed, lse, grad_mixed, HEADS // 2, HEADS // 2, parts)
    shared = [go.share(grads[1 + step], go.holders - step) for step in range(1, go.holders)]
    sum_q, _ = scatter(normed, grads[0], True)
    first = sum_q.advance(grads[1])
    first = sum_up.advance(first, after=grads[:1])
    grad_kv = first.astype(F32)
    for value in shared:
        grad_kv = grad_kv + value.astype(F32)
    grad_kv = grad_kv.astype(BF16)
    sum_kv, _ = scatter(normed, grad_kv, False)
    grad_kv = sum_kv.advance(grad_kv)
    grad_kv = sum_down.advance(grad_kv)
    grad_kv = sum_q.advance(grad_kv)
    grad_kv = sum_proj.advance(grad_kv)
    grad_qkv = jnp.concatenate([grads[0], grad_kv], axis=1)
    grad_one = back(grad_qkv, w_qkv, F32)
    grad_one = sum_kv.advance(grad_one, after=(grad_one,))
    grad_one, grad_gain_attn, grad_bias_attn = attn_norm_back(grad_one)
    grad_one = grad_one + grad_two
    grad_b_skip = jnp.sum(grad_one, axis=0)
    skip_in = grad_one.astype(BF16)
    skip_here = go.back(skip_in[:block], skip_in[block:])
    sum_skip, _ = scatter(joined, skip_in, True)
    sum_skip.advance()
    down_done = sum_down.finish()
    line.append(down_done)
    vectors = (
        grad_b_skip,
        grad_gain_attn,
        grad_bias_attn,
        grad_b_proj,
        grad_gain_mlp,
        grad_bias_mlp,
        grad_b_up,
        grad_b_down,
        grad_gain_head,
        grad_bias_head,
        grad_w_head,
    )
    whole = jnp.concatenate([grad_b_head, grad_w_conv.reshape(-1), grad_b_conv])
    packed = [v.reshape(devices, -1) for v in vectors]
    packed.append(jnp.broadcast_to(whole[None], (devices, whole.shape[0])))
    packed = jnp.concatenate(packed, axis=1)
    tile = 8 * LANES
    packed = jnp.pad(packed, ((0, 0), (0, -packed.shape[1] % tile)))
    packed = packed.reshape(-1, LANES)
    sum_small = Scatter(line, packed, True, F32)
    sum_small.advance()
    sum_up.advance()
    sum_q.advance()
    sum_skip.advance()
    sum_small.advance()
    sum_kv.advance()
    skip_here = lax.optimization_barrier((skip_here, *line))[0]
    grad_joined = back_project(skip_here.reshape(rows, width), w_skip).reshape(2, block, 2 * width)
    image_shape = image_tokens.shape
    grad_image = grad_joined[:, :image_dev, :width].reshape(image_shape)
    grad_image_skip = grad_joined[:, :image_dev, width:].reshape(image_shape)
    grad_text = grad_joined[:, image_dev : image_dev + text_dev, :width]
    grad_text_skip = grad_joined[:, image_dev : image_dev + text_dev, width:]

    sum_proj.advance()
    sum_q.advance()
    sum_skip.advance()
    sum_small.advance()
    sum_kv.advance()
    sum_skip.advance()
    sum_small.advance()
    up_done, proj_done = sum_up.finish(), sum_proj.finish()
    q_done, kv_done, skip_done = sum_q.finish(), sum_kv.finish(), sum_skip.finish()
    packed = sum_small.finish().reshape(-1)
    small = []
    start = 0
    for v in vectors:
        size = v.size // devices
        small.append(packed[start : start + size])
        start += size
    small[-1] = small[-1].reshape(-1, grad_w_head.shape[1])
    whole = packed[start : start + whole.shape[0]]
    patch_size = grad_b_head.shape[0]
    taps = grad_w_conv.size
    return (
        prediction,
        text_out,
        grad_image,
        grad_text,
        grad_image_skip,
        grad_text_skip,
        skip_done,
        small[0],
        small[1],
        small[2],
        jnp.concatenate([q_done, kv_done], axis=1),
        proj_done,
        small[3],
        small[4],
        small[5],
        up_done,
        small[6],
        down_done,
        small[7],
        small[8],
        small[9],
        small[10],
        whole[:patch_size],
        whole[patch_size : patch_size + taps].reshape(LAT_CH, LAT_CH, 3, 3),
        whole[patch_size + taps :],
    )


def solution(mesh):
    rows = P(("gx", "gy"))
    image = P("gx", None, "gy", None)
    text = P("gx", "gy", None)
    latent = P("gx", None, None, "gy")
    return jax.shard_map(
        per_device,
        mesh=mesh,
        in_specs=(image, text, image, text, P("gx"), P("gx"), latent, text) + (P(),) * 19,
        out_specs=(latent, text, image, text, image, text) + (rows,) * 16 + (P(),) * 3,
        check_vma=False,
    )
```
